32 devices in a mesh: grp: 4 (over y, x), gx: 2 (over core), gy: 4 (over z).
Axes of the slice: x: 2, y: 2, z: 4, core: 2. Of those that a mesh axis runs over, the one named last changes fastest.
Arguments:
- pressure: float32 [4, 8, 64, 128], P('grp', 'gx', 'gy'), may hold values from -6 to 6
- source: float32 [4, 8, 64, 128], P('grp', 'gx', 'gy'), may hold values from -6 to 6
- storage: float32 [4, 8, 64, 128], P('grp', 'gx', 'gy'), may hold values from 0.05 to 2
- well_mask: int32 [4, 8, 64, 128], P('grp', 'gx', 'gy'), may hold values 0 or 1
- block_id: int32 [4, 8, 64, 128], P('grp', 'gx', 'gy'), may hold values from 0 to 63
- basis_weight: float32 [4, 8, 8, 64, 128], P('grp', None, 'gx', 'gy'), may hold values from 0 to 1
- host_elem: int32 [4, 8, 64, 128], P('grp', 'gx', 'gy'), may hold values from 0 to 8191
- displacement: float32 [4, 3, 8, 64, 128], P('grp', None, 'gx', 'gy'), may hold values from -4 to 4
- body_force: float32 [4, 3, 8, 64, 128], P('grp', None, 'gx', 'gy'), may hold values from -6 to 6
- modulus: float32 [4, 8, 64, 128], P('grp', 'gx', 'gy'), may hold values from 0.5 to 4
- elem_mask: int32 [4, 8, 64, 128], P('grp', 'gx', 'gy'), may hold values 0 or 1
- stiffness: float32 [24, 24], replicated, as said below
Outputs:
- pressure_out: float32 [4, 8, 64, 128], P('grp', 'gx', 'gy')
- displacement_out: float32 [4, 3, 8, 64, 128], P('grp', None, 'gx', 'gy')
The draws below stay inside these ranges and needn't reach their ends.
Inputs may be any that keep to these rules, and one draw needn't show every extreme that they name: stiffness is symmetric and each diagonal entry exceeds the sum of the magnitudes of the other entries in its row by one.
All inputs are finite; a program needn't handle non-finite values. No bound on the sum of `well_mask` or of `elem_mask` on one device may be relied on, other than what follows from the above.
Results may differ from the reference program's by a relative error of at most 0.0003.
Values sent between devices are 32-bit elements; how exact they have to be, the bound alone decides.
No kernel may reach another device: no remote copies, remote signals or barrier semaphores. Data moves between devices by JAX's collectives and lax.ppermute only.
A program may use at most 64 MiB of HBM per device.

```python
import math
import jax
import jax.numpy as jnp
from jax import lax

FX = 4
FY = 16
FZ = 128
NBLK = 64
SWEEPS = 2
ITERS = 2
NXF = 8
NYF = 64
N_GRP = 4
N_GX = 2
N_GY = 4


def draw_stiffness(key, part):
    random_part = jax.random.normal(jax.random.fold_in(key, 11), (24, 24), jnp.float32) * 0.3
    paired = (random_part + random_part.T) * 0.7071
    identity = jnp.eye(24, dtype=jnp.float32)
    offdiag = paired * (1.0 - identity)
    dominant = jnp.sum(jnp.abs(offdiag), axis=1) + 1.0
    return offdiag + identity * dominant[:, None]


def with_ends(drawn, stream_key, low, largest):
    longest = drawn.shape.index(max(drawn.shape))
    spots = []
    for shift in (0, 1):
        where = [jax.random.randint(jax.random.fold_in(stream_key, axis), (), 0, length) for axis, length in enumerate(drawn.shape)]
        where[longest] = (where[longest] + shift) % drawn.shape[longest]
        spots.append(tuple(where))
    return drawn.at[spots[0]].set(low).at[spots[1]].set(largest)


def steps_of(stream_key, shape, shards, low, high):
    def one(dim, blocks):
        heights = jax.random.uniform(jax.random.fold_in(jax.random.fold_in(stream_key, 6), dim), (blocks,), jnp.float32, low / len(shards), high / len(shards))
        return jnp.repeat(jnp.exp(heights), shape[dim] // blocks).reshape((-1,) + (1,) * (len(shape) - dim - 1))

    loudness = one(*shards[0])
    for cut in shards[1:]:
        loudness = loudness * one(*cut)
    return loudness


def centred(own_key, dims, deviation, limit, split=(), kind=jnp.bfloat16):
    drawn = jax.random.normal(own_key, dims, jnp.float32) * deviation
    if len(split) > 0:
        drawn = steps_of(own_key, dims, split, -0.22, 0.18) * drawn
    return jnp.clip(drawn, min=-limit, max=limit).astype(kind)


def setup_inputs(seed: int = 0) -> dict:
    seeds = jax.random.split(jax.random.key(seed), 13)
    pressure = centred(seeds[0], (N_GRP, NXF, NYF, FZ), 1.0, 6.0, ((0, 4), (1, 2), (2, 4)), jnp.float32)
    source = centred(seeds[1], (N_GRP, NXF, NYF, FZ), 1.0, 6.0, ((0, 4), (1, 2), (2, 4)), jnp.float32)
    storage = jnp.clip(jnp.exp(math.log(2.0) - 3.6888794 * jax.random.uniform(seeds[2], (N_GRP, NXF, NYF, FZ), jnp.float32) ** steps_of(seeds[2], (N_GRP, NXF, NYF, FZ), ((0, 4), (1, 2), (2, 4)), -0.2, 0.2)), 0.05, 2.0)
    well_mask = with_ends((jax.random.randint(seeds[3], (N_GRP, NXF, NYF, FZ), 0, 16) < 1).astype(jnp.int32), jax.random.fold_in(seeds[3], 1), 0, 1)
    block_id = with_ends(jax.random.randint(seeds[4], (N_GRP, NXF, NYF, FZ), 0, NBLK), jax.random.fold_in(seeds[4], 1), 0, NBLK - 1).astype(jnp.int32)
    basis_weight = jnp.clip(1.0 * jax.random.uniform(seeds[5], (N_GRP, 8, NXF, NYF, FZ), jnp.float32) ** steps_of(seeds[5], (N_GRP, 8, NXF, NYF, FZ), ((0, 4), (2, 2), (3, 4)), -0.2, 0.2), 0.0, 1.0)
    host_elem = with_ends(jax.random.randint(seeds[6], (N_GRP, NXF, NYF, FZ), 0, FX * FY * FZ), jax.random.fold_in(seeds[6], 1), 0, (FX * FY * FZ) - 1).astype(jnp.int32)
    displacement = centred(seeds[7], (N_GRP, 3, NXF, NYF, FZ), 0.3, 4.0, ((0, 4), (2, 2), (3, 4)), jnp.float32)
    body_force = centred(seeds[8], (N_GRP, 3, NXF, NYF, FZ), 1.0, 6.0, ((0, 4), (2, 2), (3, 4)), jnp.float32)
    modulus = jnp.clip(jnp.exp(math.log(4.0) - 2.0794415 * jax.random.uniform(seeds[9], (N_GRP, NXF, NYF, FZ), jnp.float32) ** steps_of(seeds[9], (N_GRP, NXF, NYF, FZ), ((0, 4), (1, 2), (2, 4)), -0.2, 0.2)), 0.5, 4.0)
    elem_mask = with_ends((jax.random.randint(seeds[10], (N_GRP, NXF, NYF, FZ), 0, 8) < 7).astype(jnp.int32), jax.random.fold_in(seeds[10], 1), 0, 1)
    stiffness = draw_stiffness(jax.random.fold_in(seeds[12], 71), 0)
    return dict(pressure=pressure, source=source, storage=storage, well_mask=well_mask, block_id=block_id, basis_weight=basis_weight, host_elem=host_elem, displacement=displacement, body_force=body_force, modulus=modulus, elem_mask=elem_mask, stiffness=stiffness)


biot_coef = 1.5
relaxation = 0.8
spring_coef = 0.5
well_index = 4.0
highest = lax.Precision.HIGHEST


def coupling_vector():
    index = jnp.arange(24, dtype=jnp.int32)
    corner = index // 3
    component = index % 3
    bitval = (corner >> (2 - component)) & 1
    return (bitval.astype(jnp.float32) * 2.0 - 1.0) * 0.25


def corner_list():
    return [((corner >> 2) & 1, (corner >> 1) & 1, corner & 1) for corner in range(8)]


def reference(pressure, source, storage, well_mask, block_id, basis_weight, host_elem, displacement, body_force, modulus, elem_mask, stiffness):
    layers = N_GRP - 1
    elements = FX * FY * FZ

    def to_grid(field):
        return jnp.moveaxis(field, 0, 2).reshape(NXF, NYF, layers * FZ)

    def from_grid(field):
        return jnp.moveaxis(field.reshape(NXF, NYF, layers, FZ), 2, 0)

    def to_tiles(field):
        return field.reshape(layers, N_GX, FX, N_GY, FY, FZ).transpose(0, 1, 3, 2, 4, 5).reshape(-1)

    def from_tiles(flat):
        return flat.reshape(layers, N_GX, N_GY, FX, FY, FZ).transpose(0, 1, 3, 2, 4, 5).reshape(layers, NXF, NYF, FZ)

    def to_blocks(field):
        return field.reshape(N_GX, FX, N_GY, FY, FZ).transpose(0, 2, 1, 3, 4).reshape(-1)

    def from_blocks(flat):
        return flat.reshape(N_GX, N_GY, FX, FY, FZ).transpose(0, 2, 1, 3, 4).reshape(NXF, NYF, FZ)

    columns = (jnp.arange(N_GX, dtype=jnp.int32)[:, None] * N_GY + jnp.arange(N_GY, dtype=jnp.int32)[None, :]).astype(jnp.int32)
    host_tiles = to_tiles(host_elem[:layers]).reshape(layers, N_GX, N_GY, elements)
    host_seg = (columns[None, :, :, None] * elements + host_tiles).astype(jnp.int32).reshape(-1)
    tile_ids = jnp.arange(layers * N_GX * N_GY, dtype=jnp.int32).reshape(layers, N_GX, N_GY, 1)
    block_tiles = to_tiles(block_id[:layers]).reshape(layers, N_GX, N_GY, elements)
    block_seg = (tile_ids * NBLK + block_tiles).astype(jnp.int32).reshape(-1)
    coarse_count = layers * N_GX * N_GY * NBLK

    coupling = coupling_vector()
    mech_mask = elem_mask[layers].astype(jnp.float32).reshape(-1)
    weights = modulus[layers].reshape(-1) * mech_mask

    def spread(nodes):
        padded = jnp.pad(nodes, ((0, 0), (0, 1), (0, 1), (0, 1)))
        pieces = [padded[:, shift_x:shift_x + NXF, shift_y:shift_y + NYF, shift_z:shift_z + FZ] for shift_x, shift_y, shift_z in corner_list()]
        return jnp.stack(pieces).reshape(24, -1)

    def assemble(values):
        parts = values.reshape(8, 3, NXF, NYF, FZ)
        total = jnp.zeros((3, NXF + 1, NYF + 1, FZ + 1), jnp.float32)
        for corner, (shift_x, shift_y, shift_z) in enumerate(corner_list()):
            total = total + jnp.pad(parts[corner], ((0, 0), (shift_x, 1 - shift_x), (shift_y, 1 - shift_y), (shift_z, 1 - shift_z)))
        return total[:, :NXF, :NYF, :FZ]

    def apply(vector):
        return assemble(jnp.dot(stiffness, spread(vector), precision=highest) * weights[None, :]) + spring_coef * vector

    initial = displacement[layers]
    strain = mech_mask * jnp.dot(coupling, spread(initial), precision=highest)
    strain_cells = to_grid(from_tiles(to_blocks(strain.reshape(NXF, NYF, FZ))[host_seg]))

    start = to_grid(pressure[:layers])
    diagonal = 6.0 + to_grid(storage[:layers]) + well_index * to_grid(well_mask[:layers].astype(jnp.float32))
    forcing = to_grid(source[:layers]) - biot_coef * strain_cells

    def neighbours(field):
        padded = jnp.pad(field, 1)
        total = padded[2:, 1:-1, 1:-1] + padded[:-2, 1:-1, 1:-1]
        total = total + padded[1:-1, 2:, 1:-1] + padded[1:-1, :-2, 1:-1]
        return total + padded[1:-1, 1:-1, 2:] + padded[1:-1, 1:-1, :-2]

    def residual(field):
        return forcing - (diagonal * field - neighbours(field))

    current = start
    for sweep_index in range(SWEEPS):
        current = current + relaxation * residual(current) / diagonal
    remainder = to_tiles(from_grid(residual(current)))
    weight_flat = jnp.stack([to_tiles(basis_weight[:layers, index]) for index in range(8)])
    diag_flat = to_tiles(from_grid(diagonal))
    coarse = jax.ops.segment_sum((weight_flat * remainder).T, block_seg, num_segments=coarse_count)
    scale = 1.0 + jax.ops.segment_sum((weight_flat * weight_flat * diag_flat).T, block_seg, num_segments=coarse_count)
    correction = coarse / scale
    delta = jnp.sum(weight_flat.T * correction[block_seg], axis=1)
    updated = current + to_grid(from_tiles(delta))

    change = to_tiles(from_grid(updated - start))
    sums = jax.ops.segment_sum(change, host_seg, num_segments=N_GX * N_GY * elements)
    counts = jax.ops.segment_sum(jnp.ones_like(change), host_seg, num_segments=N_GX * N_GY * elements)
    element_pressure = from_blocks(sums / jnp.maximum(counts, 1.0)).reshape(-1)
    force = body_force[layers] + biot_coef * assemble(coupling[:, None] * (mech_mask * element_pressure)[None, :])

    solution = initial
    remain = force - apply(solution)
    search = remain
    norm_now = jnp.sum(remain * remain)
    for iteration in range(ITERS):
        image = apply(search)
        step_size = norm_now / jnp.sum(search * image)
        solution = solution + step_size * search
        remain = remain - step_size * image
        norm_next = jnp.sum(remain * remain)
        search = remain + (norm_next / norm_now) * search
        norm_now = norm_next
    pressure_out = jnp.concatenate([from_grid(updated), jnp.zeros((1, NXF, NYF, FZ), jnp.float32)], 0)
    displacement_out = jnp.concatenate([jnp.zeros((layers, 3, NXF, NYF, FZ), jnp.float32), solution[None]], 0)
    return pressure_out, displacement_out
```

```python
import functools
import jax
import jax.numpy as jnp
from jax import lax
from jax.experimental import pallas as pl
from jax.experimental.pallas import tpu as pltpu
from jax.sharding import PartitionSpec as P

NBLK = 64

biot_coef = 1.5
relaxation = 0.8
spring_coef = 0.5
well_index = 4.0

H = 3
TOP = 8
f32 = jnp.float32
bf16 = jnp.bfloat16


def pairs_a(n):
    return [(i, i ^ 1) for i in range(n)]


def pairs_b(n):
    return [(i, (i + 1) % n if i % 2 else (i - 1) % n) for i in range(n)]


def swap_a(value, axis):
    return lax.ppermute(value, axis, pairs_a(lax.axis_size(axis)))


def swap_b(value, axis):
    return lax.ppermute(value, axis, pairs_b(lax.axis_size(axis)))


def both(value_a, value_b, axis):
    got_a = swap_a(value_a, axis)
    if lax.axis_size(axis) == 2:
        return got_a, got_a
    return got_a, swap_b(value_b, axis)


def by_xor(value, axis):
    n = lax.axis_size(axis)
    return [lax.ppermute(value, axis, [(i, i ^ k) for i in range(n)]) for k in range(1, n)]


def call(body, name, outs, *args, scratch=()):
    vmem = pl.BlockSpec(memory_space=pltpu.VMEM)
    unique, spots = [], []
    for arg in args:
        found = [i for i, other in enumerate(unique) if other is arg]
        if not found:
            unique.append(arg)
        spots.append(found[0] if found else len(unique) - 1)

    def expanded(*refs):
        return body(*[refs[i] for i in spots], *refs[len(unique) :])

    return pl.pallas_call(
        expanded,
        name=name,
        out_shape=[jax.ShapeDtypeStruct(o, f32) for o in outs],
        in_specs=[vmem] * len(unique),
        out_specs=[vmem] * len(outs),
        scratch_shapes=list(scratch),
    )(*unique)


class Place:
    def __init__(self):
        self.groups = lax.axis_size("grp")
        self.g = lax.axis_index("grp")
        self.mech = self.g == self.groups - 1
        for name in ("x", "y"):
            n, i = lax.axis_size("g" + name), lax.axis_index("g" + name)
            setattr(self, name + "odd", lax.rem(i, 2) == 1)
            setattr(self, name + "prev", i > 0)
            setattr(self, name + "next", i < n - 1)


def lane(shape):
    return lax.broadcasted_iota(jnp.int32, shape, len(shape) - 1)


def sub(shape):
    return lax.broadcasted_iota(jnp.int32, shape, len(shape) - 2)


def roll(value, shift, axis):
    return pltpu.roll(value, shift % value.shape[axis], axis)


def z_up(value):
    n = value.shape[-1]
    return jnp.where(lane(value.shape) < n - 1, roll(value, -1, value.ndim - 1), 0.0)


def z_down(value):
    return jnp.where(lane(value.shape) > 0, roll(value, 1, value.ndim - 1), 0.0)


def y_up(value):
    return roll(value, -1, value.ndim - 2)


def y_down(value):
    return roll(value, 1, value.ndim - 2)


def pack_rows(at, tile, out_a, out_b, fields, size_x, size_y):
    for f in range(fields):
        for x in range(size_x):
            low = tile[f, x, 0:H, :]
            high = tile[f, x, size_y - H : size_y, :]
            r = (f * size_x + x) * H
            out_a[r : r + H, :] = jnp.where(at.yodd, low, high)
            out_b[r : r + H, :] = jnp.where(at.yodd, high, low)


def extend(at, ext, tile, xa, xb, ya, yb, xya, xyb, fields, size_x, size_y):
    rows = ext.shape[2]
    lanes = ext.shape[3]
    blank_low = jnp.zeros((TOP, lanes), f32)
    blank_high = jnp.zeros((rows - TOP - size_y, lanes), f32)

    def side(valid, odd_is, a, b, index):
        value = jnp.where(odd_is, a[index], b[index])
        return jnp.where(valid, value, 0.0)

    def fill(f, xe, xs, valid, own, msg_a, msg_b):
        ext[f, xe, 0:TOP, :] = blank_low
        ext[f, xe, TOP + size_y : rows, :] = blank_high
        ext[f, xe, TOP : TOP + size_y, :] = own
        r = (f * size_x + xs) * H
        index = (slice(r, r + H), slice(None))
        before = side(valid & at.yprev, at.yodd, msg_a, msg_b, index)
        after = side(valid & at.ynext, ~at.yodd, msg_a, msg_b, index)
        ext[f, xe, TOP - H : TOP, :] = before
        ext[f, xe, TOP + size_y : TOP + size_y + H, :] = after

    class Mixed:
        def __init__(self, pick_a, a, b):
            self.pick_a, self.a, self.b = pick_a, a, b

        def __getitem__(self, index):
            if self.a is self.b:
                return self.a[index]
            return jnp.where(self.pick_a, self.a[index], self.b[index])

    always = at.g >= 0
    for f in range(fields):
        for x in range(size_x):
            fill(f, H + x, x, always, tile[f, x], ya, yb)
        for k in range(H):
            xs = size_x - H + k
            tile_p = Mixed(at.xodd, xa, xb)
            own = jnp.where(at.xprev, tile_p[f, xs], 0.0)
            fill(f, k, xs, at.xprev, own, Mixed(at.xodd, xya[0], xyb[0]), Mixed(at.xodd, xya[1], xyb[1]))
            tile_n = Mixed(~at.xodd, xa, xb)
            own = jnp.where(at.xnext, tile_n[f, k], 0.0)
            fill(f, H + size_x + k, k, at.xnext, own, Mixed(~at.xodd, xya[0], xyb[0]), Mixed(~at.xodd, xya[1], xyb[1]))


def corners(nodes, x):
    out = [None] * 24
    for a in range(2):
        for m in range(3):
            here = nodes[m, x + a]
            up = z_up(here)
            for e, v in ((0, here), (1, up)):
                out[3 * (4 * a + e) + m] = v
                out[3 * (4 * a + 2 + e) + m] = y_up(v)
    return out


def stack_tiles(values, tiles):
    cols = [jnp.concatenate([v[8 * t : 8 * t + 8] for v in values], axis=0) for t in tiles]
    return jnp.concatenate(cols, axis=1)


def split(value):
    high = value.astype(bf16)
    return high, (value - high.astype(f32)).astype(bf16)


def stiff(k_high, k_low, stacked):
    high, low = split(stacked)
    dot = functools.partial(jnp.dot, preferred_element_type=f32)
    return dot(k_high[...], high) + dot(k_high[...], low) + dot(k_low[...], high)


def add_apply(nodes, weight, out, k_high, k_low, first, last):
    rows = nodes.shape[2]
    tiles = rows // 8
    for m in range(3):
        out[m, first] = jnp.zeros((rows, 128), f32)

    def plane(x, carry):
        v = stiff(k_high, k_low, stack_tiles(corners(nodes, x), range(tiles)))
        w = weight[x]

        def entry(j):
            return w * jnp.concatenate(
                [v[8 * j : 8 * j + 8, 128 * t : 128 * t + 128] for t in range(tiles)], axis=0
            )

        for a in range(2):
            for m in range(3):
                part = []
                for b in range(2):
                    c = 4 * a + 2 * b
                    part.append(entry(3 * c + m) + z_down(entry(3 * (c + 1) + m)))
                total = part[0] + y_down(part[1])
                if a == 0:
                    out[m, x] = out[m, x] + total
                else:
                    out[m, x + 1] = total
        return carry

    lax.fori_loop(first, last, plane, 0)


def total_of(value):
    return jnp.sum(jnp.sum(value, axis=0, keepdims=True), axis=1, keepdims=True)


def onehot_sum(rows_of, size_x, size_y, shape, row_fn):
    def plane(x, acc):
        lefts, rights = [], []
        for y in range(size_y):
            left, right = row_fn(x, y)
            lefts.append(left)
            rights.append(right)
        return acc + lax.dot_general(
            jnp.concatenate(lefts, axis=1),
            jnp.concatenate(rights, axis=1),
            (((1,), (1,)), ((), ())),
            preferred_element_type=f32,
        )

    return lax.fori_loop(0, size_x, plane, jnp.zeros(shape, f32))


def z_slot(field, x, size_x):
    return 8 * (field * size_x + x)


def pack_body(p, src, sto, well, host, u, body, mod, mask, tile, ya, yb, zmsg):
    at = Place()
    size_x, size_y = p.shape[0], p.shape[1]

    @pl.when(at.mech)
    def _():
        tile[0:3] = u[...]
        tile[3:6] = body[...]
        tile[6] = mod[...] * mask[...].astype(f32)
        pack_rows(at, tile, ya, yb, 7, size_x, size_y)

    @pl.when(~at.mech)
    def _():
        where = lane((size_y, 128))
        msg = jnp.zeros((size_y, 128), f32)
        for x in range(size_x):
            diag = 6.0 + sto[x] + well_index * well[x].astype(f32)
            for f, v in enumerate((p[x], relaxation / diag, src[x], host[x].astype(f32))):
                s = z_slot(f, x, size_x)
                msg = jnp.where((where >= s) & (where < s + 6), roll(v, s + 3, 1), msg)
        zmsg[...] = msg


def strain_body(tile, xa, xb, ya, yb, xyaa, xyab, xyba, xybb, mask, host, zmsg, out, ue):
    at = Place()
    size_x, size_y = mask.shape[0], mask.shape[1]
    rows = size_x * size_y

    @pl.when(at.mech)
    def _():
        for m in range(3):
            for x in range(size_x + 1):
                r = (m * size_x + (x if x < size_x else 0)) * H
                if x < size_x:
                    own = tile[m, x]
                    after = jnp.where(at.yodd, yb[r : r + 1, :], ya[r : r + 1, :])
                else:
                    own = jnp.where(at.xodd, xb[m, 0], xa[m, 0])
                    of_a = jnp.where(at.yodd, xyab[r : r + 1, :], xyaa[r : r + 1, :])
                    of_b = jnp.where(at.yodd, xybb[r : r + 1, :], xyba[r : r + 1, :])
                    after = jnp.where(at.xodd, of_b, of_a)
                    own = jnp.where(at.xnext, own, 0.0)
                    after = jnp.where(at.xnext, after, 0.0)
                ue[m, x, 0:size_y, :] = own
                ue[m, x, size_y : size_y + 8, :] = jnp.zeros((8, 128), f32)
                ue[m, x, size_y : size_y + 1, :] = jnp.where(at.ynext, after, 0.0)
        before = None
        for x in range(size_x + 1):
            v = ue[0, x]
            s = v + z_up(v)
            q0 = s + y_up(s)
            v = ue[1, x]
            s = v + z_up(v)
            q1 = y_up(s) - s
            v = ue[2, x]
            s = z_up(v) - v
            q2 = s + y_up(s)
            if x:
                value = (q0 - before[0]) + (q1 + before[1]) + (q2 + before[2])
                r = (x - 1) * size_y
                out[r : r + size_y, :] = 0.25 * mask[x - 1].astype(f32) * value[0:size_y]
            before = (q0, q1, q2)

    @pl.when(~at.mech)
    def _():
        high_id, low_id = sub((rows, 128)), sub((128, 128))

        def row(x, y):
            h = host[x, y : y + 1, :]
            left = jnp.where(high_id == (h >> 7), 1.0, 0.0).astype(bf16)
            right = jnp.where(low_id == (h & 127), 1.0, 0.0).astype(bf16)
            return left, right

        out[0:rows, :] = onehot_sum(None, size_x, size_y, (rows, 128), row)
        out[rows : rows + size_y, :] = zmsg[...]


def gather_body(*refs):
    at = Place()
    k = at.groups - 1
    got, refs = refs[:k], refs[k:]
    p, src, sto, well, host = refs[:5]
    tile, xa, xb, ya, yb, xyaa, xyab, xyba, xybb, k_high, k_low = refs[5:16]
    out, out_a, out_b, g0, we, ext, acc, table = refs[16:]
    size_x, size_y = p.shape[0], p.shape[1]
    rows = size_x * size_y

    def pick(partner, index):
        value = got[0][index]
        for i in range(1, k):
            value = jnp.where((at.g ^ partner) == i + 1, got[i][index], value)
        return value

    @pl.when(~at.mech)
    def _():
        table[...] = pick(at.groups - 1, (slice(0, rows), slice(None)))
        zrows = (slice(rows, rows + size_y), slice(None))
        before = jnp.where(at.g > 0, pick(at.g - 1, zrows), 0.0)
        after = jnp.where(at.g < at.groups - 2, pick(at.g + 1, zrows), 0.0)
        spot = lane((size_y, 128))
        zside = jnp.where((spot & 7) < 3, before, after)
        first_host = z_slot(3, 0, size_x)
        zhost = jnp.where(spot >= first_host, zside, 0.0).astype(jnp.int32)
        cells = [host[x] for x in range(size_x)] + [zhost]
        cells = [c[8 * t : 8 * t + 8] for c in cells for t in range(size_y // 8)]
        highs = [c >> 7 for c in cells]
        lows = [c & 127 for c in cells]

        def step(h, values):
            line = jnp.broadcast_to(table[pl.ds(h, 1), :], (8, 128))
            return tuple(
                jnp.where(hi == h, jnp.take_along_axis(line, lo, axis=1, mode="promise_in_bounds"), v)
                for hi, lo, v in zip(highs, lows, values)
            )

        values = lax.fori_loop(0, rows, step, tuple(jnp.zeros((8, 128), f32) for _ in cells), unroll=4)
        per = size_y // 8
        strain = [jnp.concatenate(values[per * i : per * i + per], axis=0) for i in range(size_x + 1)]

        def z_tile(field, x, depth, source):
            value = roll(source, -(z_slot(field, x, size_x) + 3), 1)
            return jnp.where((spot < depth) | (spot >= 128 - depth), value, 0.0)

        for x in range(size_x):
            diag = 6.0 + sto[x] + well_index * well[x].astype(f32)
            out[0, x, :, 0:128] = p[x]
            out[0, x, :, 128:256] = z_tile(0, x, 3, zside)
            out[1, x, :, 0:128] = relaxation / diag
            out[1, x, :, 128:256] = z_tile(1, x, 2, zside)
            out[2, x, :, 0:128] = src[x] - biot_coef * strain[x]
            out[2, x, :, 128:256] = z_tile(2, x, 2, zside) - biot_coef * z_tile(3, x, 2, strain[size_x])
        pack_rows(at, out, out_a, out_b, 3, size_x, size_y)

    @pl.when(at.mech)
    def _():
        extend(at, ext, tile, xa, xb, ya, yb, (xyaa, xyab), (xyba, xybb), 7, size_x, size_y)
        we[...] = ext[6]
        add_apply(ext, we, acc, k_high, k_low, 1, size_x + 5)
        for m in range(3):
            for x in range(2, size_x + 5):
                g0[m, x] = ext[3 + m, x] - acc[m, x] - spring_coef * ext[m, x]


def flow_body(tile, xa, xb, ya, yb, xyaa, xyab, xyba, xybb, sto, well, block, basis, host, pressure, sums, ext, work, corr):
    at = Place()
    size_x, size_y = sto.shape[0], sto.shape[1]
    rows = size_x * size_y
    nx = size_x + 2 * H

    @pl.when(at.mech)
    def _():
        pressure[...] = jnp.zeros_like(pressure)

    @pl.when(~at.mech)
    def _():
        extend(at, ext, tile, xa, xb, ya, yb, (xyaa, xyab), (xyba, xybb), 3, size_x, size_y)

        def around(field, x):
            v = field[x]
            total = field[x + 1] + field[x - 1]
            total = total + y_up(v) + y_down(v)
            return total + roll(v, 1, 1) + roll(v, -1, 1)

        p0 = [ext[0, x] for x in range(nx)]
        p1 = [None] * nx
        for x in range(1, nx - 1):
            p1[x] = (1.0 - relaxation) * p0[x] + ext[1, x] * (ext[2, x] + around(p0, x))
        p2 = [None] * nx
        for x in range(2, nx - 2):
            p2[x] = (1.0 - relaxation) * p1[x] + ext[1, x] * (ext[2, x] + around(p1, x))
        own = slice(TOP, TOP + size_y)
        for x in range(size_x):
            r = slice(x * size_y, (x + 1) * size_y)
            diag = 6.0 + sto[x] + well_index * well[x].astype(f32)
            here = p2[x + H]
            res = (ext[2, x + H] + around(p2, x + H))[own, 0:128] - diag * here[own, 0:128]
            work[0, r, :] = here[own, 0:128]
            work[1, r, :] = res
            work[2, r, :] = diag
        block_ids = sub((NBLK, 128))

        def coarse_row(x, y):
            r = x * size_y + y
            w = basis[pl.ds(r, 8, stride=rows), :]
            res = work[1, pl.ds(r, 1), :]
            diag = work[2, pl.ds(r, 1), :]
            high, low = split(jnp.concatenate([w * res, w * w * diag], axis=0))
            right = jnp.where(block_ids == block[x, y : y + 1, :], 1.0, 0.0).astype(bf16)
            return jnp.concatenate([high, low], axis=0), right

        acc = onehot_sum(None, size_x, size_y, (32, NBLK), coarse_row)
        corr[...] = jnp.zeros_like(corr)
        corr[:, 0:NBLK] = (acc[0:8] + acc[16:24]) / (1.0 + (acc[8:16] + acc[24:32]))
        lines = [jnp.broadcast_to(corr[j : j + 1, :], (8, 128)) for j in range(8)]
        for x in range(size_x):
            for t in range(size_y // 8):
                ids = block[x, 8 * t : 8 * t + 8, :]
                r = x * size_y + 8 * t
                delta = jnp.zeros((8, 128), f32)
                for j in range(8):
                    got = jnp.take_along_axis(lines[j], ids, axis=1, mode="promise_in_bounds")
                    delta = delta + basis[j * rows + r : j * rows + r + 8, :] * got
                updated = work[0, r : r + 8, :] + delta
                pressure[x, 8 * t : 8 * t + 8, :] = updated
                change = updated - tile[0, x, 8 * t : 8 * t + 8, 0:128]
                high = change.astype(bf16).astype(f32)
                work[0, r : r + 8, :] = high
                work[1, r : r + 8, :] = change - high
        high_id, low_id = sub((rows, 128)), sub((128, 128))

        def sum_row(x, y):
            r = x * size_y + y
            h = host[x, y : y + 1, :]
            hit = high_id == (h >> 7)
            left = [jnp.where(hit, work[i, pl.ds(r, 1), :], 0.0).astype(bf16) for i in range(2)]
            right = jnp.where(low_id == (h & 127), 1.0, 0.0).astype(bf16)
            return jnp.concatenate(left, axis=0), right

        acc = onehot_sum(None, size_x, size_y, (2 * rows, 128), sum_row)
        sums[...] = acc[0:rows] + acc[rows : 2 * rows]


def element_body(*refs):
    at = Place()
    k = at.groups - 1
    sums, counts, refs = refs[:k], refs[k : 2 * k], refs[2 * k :]
    mask, out, out_a, out_b = refs
    size_x, size_y = mask.shape[0], mask.shape[1]

    @pl.when(at.mech)
    def _():
        for x in range(size_x):
            r = slice(x * size_y, (x + 1) * size_y)
            total = sums[0][r, :]
            count = counts[0][r, :]
            for i in range(1, k):
                total = total + sums[i][r, :]
                count = count + counts[i][r, :]
            out[0, x] = mask[x].astype(f32) * (total / jnp.maximum(count, 1.0))
        pack_rows(at, out, out_a, out_b, 1, size_x, size_y)


def krylov_body(tile, xa, xb, ya, yb, xyaa, xyab, xyba, xybb, g0, we, k_high, k_low, r_out, q_out, scal, ext, res, acc):
    at = Place()
    size_x, size_y = tile.shape[1], tile.shape[2]
    rows = ext.shape[2]
    own = slice(TOP, TOP + size_y)

    @pl.when(at.mech)
    def _():
        extend(at, ext, tile, xa, xb, ya, yb, (xyaa, xyab), (xyba, xybb), 1, size_x, size_y)
        line = sub((rows, 128))
        inside = ((line >= TOP) | at.yprev) & ((line < TOP + size_y) | at.ynext)

        def inside_x(x):
            if x < H:
                return inside & at.xprev
            if x >= H + size_x:
                return inside & at.xnext
            return inside

        before = None
        for x in range(1, size_x + 5):
            e = ext[0, x]
            sz = e + z_down(e)
            ssz = sz + y_down(sz)
            dsz = y_down(sz) - sz
            dz = z_down(e) - e
            sdz = dz + y_down(dz)
            if before is not None:
                f = (before[0] - ssz, before[1] + dsz, before[2] + sdz)
                for m in range(3):
                    value = g0[m, x] + (0.25 * biot_coef) * f[m]
                    res[m, x] = jnp.where(inside_x(x), value, 0.0)
            before = (ssz, dsz, sdz)

        add_apply(res, we, acc, k_high, k_low, 2, size_x + 4)
        rr = jnp.zeros((8, 128), f32)
        rq = jnp.zeros((8, 128), f32)
        for m in range(3):
            for x in range(H, H + size_x + 1):
                q = jnp.where(inside_x(x), acc[m, x] + spring_coef * res[m, x], 0.0)
                acc[m, x] = q
                if x < H + size_x:
                    for t in range(TOP, TOP + size_y, 8):
                        v = res[m, x, t : t + 8, :]
                        rr = rr + v * v
                        rq = rq + v * q[t : t + 8]
        rr = total_of(rr)
        shift = total_of(rq) / jnp.maximum(rr, 1e-30)
        rq = jnp.zeros((8, 128), f32)
        qq = jnp.zeros((8, 128), f32)
        for m in range(3):
            for x in range(H, H + size_x + 1):
                q = acc[m, x] - shift * res[m, x]
                acc[m, x] = q
                if x < H + size_x:
                    q_out[m, x - H] = q[own]
                    r_out[m, x - H] = res[m, x, own, :]
                    for t in range(TOP, TOP + size_y, 8):
                        v = q[t : t + 8]
                        qq = qq + v * v
                        rq = rq + v * res[m, x, t : t + 8, :]
        rq, qq = total_of(rq), total_of(qq)
        tiles = range(TOP // 8, (TOP + size_y) // 8)

        def plane(x, sums):
            uq = stack_tiles(corners(acc, x), tiles)
            ur = stack_tiles(corners(res, x), tiles)
            vq = stiff(k_high, k_low, uq)
            vr = stiff(k_high, k_low, ur)
            w = jnp.concatenate([we[x, 8 * t : 8 * t + 8, :] for t in tiles], axis=1)
            out = []
            for s, u, v in zip(sums, (uq, ur, ur), (vq, vq, vr)):
                part = u * v
                t = part[0:8]
                for j in range(1, 24):
                    t = t + part[8 * j : 8 * j + 8]
                out.append(s + w * t)
            return tuple(out)

        zero = jnp.zeros((8, 128 * len(tiles)), f32)
        e11, e12, e22 = lax.fori_loop(H, H + size_x, plane, (zero, zero, zero))
        e11 = total_of(e11) + spring_coef * qq
        e12 = total_of(e12) + spring_coef * rq
        e22 = total_of(e22) + spring_coef * rr
        for i, v in enumerate((rr, shift, rq, qq, e11, e12, e22)):
            scal[i : i + 1, :] = jnp.broadcast_to(v, (1, 128))
        scal[7:8, :] = jnp.zeros((1, 128), f32)


def final_body(scals, own, r, q, u, out):
    at = Place()

    @pl.when(~at.mech)
    def _():
        out[...] = jnp.zeros_like(out)

    @pl.when(at.mech)
    def _():
        count = scals.shape[0]
        get = lambda d, i: scals[d, i : i + 1, :]
        total = lambda fn: functools.reduce(lambda a, b: a + b, [fn(d) for d in range(count)])
        rr = total(lambda d: get(d, 0))
        mean = total(lambda d: get(d, 2) + get(d, 1) * get(d, 0)) / rr

        def shifted(low, mid, high):
            def one(d):
                gap = get(d, 1) - mean
                return get(d, high) + gap * (2.0 * get(d, mid) + gap * get(d, low))

            return total(one)

        qq = shifted(0, 2, 3)
        energy = shifted(6, 5, 4)
        ratio = qq / (mean * mean * rr)
        curve = energy / (mean * mean) - ratio * ratio * mean * rr
        second = ratio * rr / curve
        gap = own[1:2, :] - mean
        by_r = 1.0 / mean + second * (ratio - gap / mean)
        by_q = -second / mean
        out[...] = u[...] + by_r[None, None] * r[...] + by_q[None, None] * q[...]


def neighbours(tile, msg_a, msg_b):
    xa, xb = both(tile, tile, "gx")
    ya, yb = both(msg_a, msg_b, "gy")
    xyaa, xyba = both(ya, ya, "gx")
    xyab, xybb = both(yb, yb, "gx")
    return (xa, xb, ya, yb, xyaa, xyab, xyba, xybb)


def local(
    pressure,
    source,
    storage,
    well_mask,
    block_id,
    basis_weight,
    host_elem,
    displacement,
    body_force,
    modulus,
    elem_mask,
    stiffness,
):
    p, src, sto, well = pressure[0], source[0], storage[0], well_mask[0]
    host, block, mask = host_elem[0], block_id[0], elem_mask[0]
    size_x, size_y, size_z = p.shape
    rows = size_x * size_y
    basis = basis_weight[0].reshape(8 * rows, size_z)
    u, body = displacement[0], body_force[0]
    nx, ny = size_x + 2 * H, size_y + 2 * TOP
    kron = (stiffness[:, None, :, None] * jnp.eye(8, dtype=f32)[None, :, None, :]).reshape(192, 192)
    k_high = lax.reduce_precision(kron, 8, 7)
    k_low = (kron - k_high).astype(bf16)
    k_high = k_high.astype(bf16)

    msg = (7 * size_x * H, size_z)
    tile, ya, yb, zmsg = call(
        pack_body,
        "pack",
        [(7, size_x, size_y, size_z), msg, msg, (size_y, size_z)],
        p, src, sto, well, host, u, body, modulus[0], mask,
    )
    near = neighbours(tile, ya, yb)
    (line,) = call(
        strain_body,
        "strain",
        [(rows + size_y, size_z)],
        tile, *near, mask, host, zmsg,
        scratch=[pltpu.VMEM((3, size_x + 1, size_y + 8, size_z), f32)],
    )
    got = by_xor(line, "grp")
    msg = (3 * size_x * H, 2 * size_z)
    cells, ya, yb, g0, we = call(
        gather_body,
        "gather",
        [(3, size_x, size_y, 2 * size_z), msg, msg, (3, nx, ny, size_z), (nx, ny, size_z)],
        *got, p, src, sto, well, host, tile, *near, k_high, k_low,
        scratch=[
            pltpu.VMEM((7, nx, ny, size_z), f32),
            pltpu.VMEM((3, nx, ny, size_z), f32),
            pltpu.VMEM((rows, size_z), f32),
        ],
    )
    near = neighbours(cells, ya, yb)
    updated, sums = call(
        flow_body,
        "flow",
        [(size_x, size_y, size_z), (rows, size_z)],
        cells, *near, sto, well, block, basis, host,
        scratch=[
            pltpu.VMEM((3, nx, ny, 2 * size_z), f32),
            pltpu.VMEM((3, rows, size_z), f32),
            pltpu.VMEM((8, size_z), f32),
        ],
    )
    summed = by_xor(sums, "grp")
    msg = (size_x * H, size_z)
    elem, ya, yb = call(
        element_body,
        "element",
        [(1, size_x, size_y, size_z), msg, msg],
        *summed, *got, mask,
    )
    near = neighbours(elem, ya, yb)
    own = (3, size_x, size_y, size_z)
    r, q, scal = call(
        krylov_body,
        "krylov",
        [own, own, (8, size_z)],
        elem, *near, g0, we, k_high, k_low,
        scratch=[
            pltpu.VMEM((1, nx, ny, size_z), f32),
            pltpu.VMEM((3, nx, ny, size_z), f32),
            pltpu.VMEM((3, nx, ny, size_z), f32),
        ],
    )
    if lax.axis_size("gx") == 2:
        duo = jnp.stack([scal, swap_a(scal, "gx")])
        scals = jnp.concatenate([duo] + by_xor(duo, "gy"))
    else:
        scals = lax.all_gather(scal, ("gx", "gy"))
    (moved,) = call(final_body, "final", [own], scals, scal, r, q, u)
    return (updated[None], moved[None])


def solution(mesh):
    cell = P("grp", "gx", "gy", None)
    deep = P("grp", None, "gx", "gy", None)
    placed = (cell, cell, cell, cell, cell, deep, cell, deep, deep, cell, cell, P())
    return jax.shard_map(
        local,
        mesh=mesh,
        in_specs=placed,
        out_specs=(cell, deep),
        check_vma=False,
    )
```

```python
import functools
import jax
import jax.numpy as jnp
from jax import lax
from jax.experimental import pallas as pl
from jax.experimental.pallas import tpu as pltpu
from jax.sharding import PartitionSpec as P

NBLK = 64

biot_coef = 1.5
relaxation = 0.8
spring_coef = 0.5
well_index = 4.0

H = 3
TOP = 8
GRANT = 16 * 1024 * 1024
f32 = jnp.float32
bf16 = jnp.bfloat16


def pairs_a(n):
    return [(i, i ^ 1) for i in range(n)]


def pairs_b(n):
    return [(i, (i + 1) % n if i % 2 else (i - 1) % n) for i in range(n)]


def swap_a(value, axis):
    return lax.ppermute(value, axis, pairs_a(lax.axis_size(axis)))


def swap_b(value, axis):
    return lax.ppermute(value, axis, pairs_b(lax.axis_size(axis)))


def both(value_a, value_b, axis):
    got_a = swap_a(value_a, axis)
    if lax.axis_size(axis) == 2:
        return got_a, got_a
    return got_a, swap_b(value_b, axis)


def by_xor(value, axis):
    n = lax.axis_size(axis)
    return [lax.ppermute(value, axis, [(i, i ^ k) for i in range(n)]) for k in range(1, n)]


def call(body, name, outs, *args, scratch=()):
    vmem = pl.BlockSpec(memory_space=pltpu.VMEM)
    unique, spots = [], []
    for arg in args:
        found = [i for i, other in enumerate(unique) if other is arg]
        if not found:
            unique.append(arg)
        spots.append(found[0] if found else len(unique) - 1)

    def expanded(*refs):
        return body(*[refs[i] for i in spots], *refs[len(unique) :])

    return pl.pallas_call(
        expanded,
        name=name,
        out_shape=[o if hasattr(o, "dtype") else jax.ShapeDtypeStruct(o, f32) for o in outs],
        in_specs=[vmem] * len(unique),
        out_specs=[vmem] * len(outs),
        scratch_shapes=list(scratch),
        compiler_params=pltpu.CompilerParams(vmem_limit_bytes=GRANT),
    )(*unique)


class Place:
    def __init__(self):
        self.groups = lax.axis_size("grp")
        self.g = lax.axis_index("grp")
        self.mech = self.g == self.groups - 1
        for name in ("x", "y"):
            n, i = lax.axis_size("g" + name), lax.axis_index("g" + name)
            setattr(self, name + "odd", lax.rem(i, 2) == 1)
            setattr(self, name + "prev", i > 0)
            setattr(self, name + "next", i < n - 1)


def lane(shape):
    return lax.broadcasted_iota(jnp.int32, shape, len(shape) - 1)


def sub(shape):
    return lax.broadcasted_iota(jnp.int32, shape, len(shape) - 2)


def roll(value, shift, axis):
    return pltpu.roll(value, shift % value.shape[axis], axis)


def z_up(value):
    n = value.shape[-1]
    return jnp.where(lane(value.shape) < n - 1, roll(value, -1, value.ndim - 1), 0.0)


def z_down(value):
    return jnp.where(lane(value.shape) > 0, roll(value, 1, value.ndim - 1), 0.0)


def y_up(value):
    return roll(value, -1, value.ndim - 2)


def y_down(value):
    return roll(value, 1, value.ndim - 2)


def pack_rows(at, tile, out_a, out_b, fields, size_x, size_y):
    for f in range(fields):
        for x in range(size_x):
            low = tile[f, x, 0:H, :]
            high = tile[f, x, size_y - H : size_y, :]
            r = (f * size_x + x) * H
            out_a[r : r + H, :] = jnp.where(at.yodd, low, high)
            out_b[r : r + H, :] = jnp.where(at.yodd, high, low)


def extend(at, ext, tile, xa, xb, ya, yb, xya, xyb, fields, size_x, size_y):
    rows = ext.shape[2]
    lanes = ext.shape[3]
    blank_low = jnp.zeros((TOP, lanes), f32)
    blank_high = jnp.zeros((rows - TOP - size_y, lanes), f32)

    def side(valid, odd_is, a, b, index):
        value = jnp.where(odd_is, a[index], b[index])
        return jnp.where(valid, value, 0.0)

    def fill(f, xe, xs, valid, own, msg_a, msg_b):
        ext[f, xe, 0:TOP, :] = blank_low
        ext[f, xe, TOP + size_y : rows, :] = blank_high
        ext[f, xe, TOP : TOP + size_y, :] = own
        r = (f * size_x + xs) * H
        index = (slice(r, r + H), slice(None))
        before = side(valid & at.yprev, at.yodd, msg_a, msg_b, index)
        after = side(valid & at.ynext, ~at.yodd, msg_a, msg_b, index)
        ext[f, xe, TOP - H : TOP, :] = before
        ext[f, xe, TOP + size_y : TOP + size_y + H, :] = after

    class Mixed:
        def __init__(self, pick_a, a, b):
            self.pick_a, self.a, self.b = pick_a, a, b

        def __getitem__(self, index):
            if self.a is self.b:
                return self.a[index]
            return jnp.where(self.pick_a, self.a[index], self.b[index])

    always = at.g >= 0
    for f in range(fields):
        for x in range(size_x):
            fill(f, H + x, x, always, tile[f, x], ya, yb)
        for k in range(H):
            xs = size_x - H + k
            tile_p = Mixed(at.xodd, xa, xb)
            own = jnp.where(at.xprev, tile_p[f, xs], 0.0)
            fill(f, k, xs, at.xprev, own, Mixed(at.xodd, xya[0], xyb[0]), Mixed(at.xodd, xya[1], xyb[1]))
            tile_n = Mixed(~at.xodd, xa, xb)
            own = jnp.where(at.xnext, tile_n[f, k], 0.0)
            fill(f, H + size_x + k, k, at.xnext, own, Mixed(~at.xodd, xya[0], xyb[0]), Mixed(~at.xodd, xya[1], xyb[1]))


def corners(nodes, x):
    out = [None] * 24
    for a in range(2):
        for m in range(3):
            here = nodes[m, x + a]
            up = z_up(here)
            for e, v in ((0, here), (1, up)):
                out[3 * (4 * a + e) + m] = v
                out[3 * (4 * a + 2 + e) + m] = y_up(v)
    return out


def stack_tiles(values, tiles):
    cols = [jnp.concatenate([v[8 * t : 8 * t + 8] for v in values], axis=0) for t in tiles]
    return jnp.concatenate(cols, axis=1)


def split(value):
    high = value.astype(bf16)
    return high, (value - high.astype(f32)).astype(bf16)


def stiff(k_high, k_low, stacked):
    high, low = split(stacked)
    dot = functools.partial(jnp.dot, preferred_element_type=f32)
    return dot(k_high[...], high) + dot(k_high[...], low) + dot(k_low[...], high)


def spread_stiffness(stiffness, k_high, k_low):
    n = 8 * stiffness.shape[0]
    pick = jnp.where(sub((n, n // 8)) // 8 == lane((n, n // 8)), 1.0, 0.0).astype(bf16)
    keep = (sub((n, n)) & 7) == (lane((n, n)) & 7)
    for term, out in zip(split(stiffness[...]), (k_high, k_low)):
        tall = jnp.dot(pick, term, preferred_element_type=f32).astype(bf16)
        wide = lax.dot_general(tall, pick, (((1,), (1,)), ((), ())), preferred_element_type=f32)
        out[...] = jnp.where(keep, wide, 0.0).astype(bf16)


def add_apply(nodes, weight, out, k_high, k_low, first, last):
    rows = nodes.shape[2]
    tiles = rows // 8
    for m in range(3):
        out[m, first] = jnp.zeros((rows, 128), f32)

    def plane(x, carry):
        v = stiff(k_high, k_low, stack_tiles(corners(nodes, x), range(tiles)))
        w = weight[x]

        def entry(j):
            return w * jnp.concatenate(
                [v[8 * j : 8 * j + 8, 128 * t : 128 * t + 128] for t in range(tiles)], axis=0
            )

        for a in range(2):
            for m in range(3):
                part = []
                for b in range(2):
                    c = 4 * a + 2 * b
                    part.append(entry(3 * c + m) + z_down(entry(3 * (c + 1) + m)))
                total = part[0] + y_down(part[1])
                if a == 0:
                    out[m, x] = out[m, x] + total
                else:
                    out[m, x + 1] = total
        return carry

    lax.fori_loop(first, last, plane, 0)


def total_of(value):
    return jnp.sum(jnp.sum(value, axis=0, keepdims=True), axis=1, keepdims=True)


def onehot_sum(rows_of, size_x, size_y, shape, row_fn):
    def plane(x, acc):
        lefts, rights = [], []
        for y in range(size_y):
            left, right = row_fn(x, y)
            lefts.append(left)
            rights.append(right)
        return acc + lax.dot_general(
            jnp.concatenate(lefts, axis=1),
            jnp.concatenate(rights, axis=1),
            (((1,), (1,)), ((), ())),
            preferred_element_type=f32,
        )

    return lax.fori_loop(0, size_x, plane, jnp.zeros(shape, f32))


def z_slot(field, x, size_x):
    return 8 * (field * size_x + x)


def pack_body(p, src, sto, well, host, u, body, mod, mask, tile, ya, yb, zmsg):
    at = Place()
    size_x, size_y = p.shape[0], p.shape[1]

    @pl.when(at.mech)
    def _():
        tile[0:3] = u[...]
        tile[3:6] = body[...]
        tile[6] = mod[...] * mask[...].astype(f32)
        pack_rows(at, tile, ya, yb, 7, size_x, size_y)

    @pl.when(~at.mech)
    def _():
        where = lane((size_y, 128))
        msg = jnp.zeros((size_y, 128), f32)
        for x in range(size_x):
            diag = 6.0 + sto[x] + well_index * well[x].astype(f32)
            for f, v in enumerate((p[x], relaxation / diag, src[x], host[x].astype(f32))):
                s = z_slot(f, x, size_x)
                msg = jnp.where((where >= s) & (where < s + 6), roll(v, s + 3, 1), msg)
        zmsg[...] = msg


def strain_body(tile, xa, xb, ya, yb, xyaa, xyab, xyba, xybb, mask, host, zmsg, out, ue):
    at = Place()
    size_x, size_y = mask.shape[0], mask.shape[1]
    rows = size_x * size_y

    @pl.when(at.mech)
    def _():
        for m in range(3):
            for x in range(size_x + 1):
                r = (m * size_x + (x if x < size_x else 0)) * H
                if x < size_x:
                    own = tile[m, x]
                    after = jnp.where(at.yodd, yb[r : r + 1, :], ya[r : r + 1, :])
                else:
                    own = jnp.where(at.xodd, xb[m, 0], xa[m, 0])
                    of_a = jnp.where(at.yodd, xyab[r : r + 1, :], xyaa[r : r + 1, :])
                    of_b = jnp.where(at.yodd, xybb[r : r + 1, :], xyba[r : r + 1, :])
                    after = jnp.where(at.xodd, of_b, of_a)
                    own = jnp.where(at.xnext, own, 0.0)
                    after = jnp.where(at.xnext, after, 0.0)
                ue[m, x, 0:size_y, :] = own
                ue[m, x, size_y : size_y + 8, :] = jnp.zeros((8, 128), f32)
                ue[m, x, size_y : size_y + 1, :] = jnp.where(at.ynext, after, 0.0)
        before = None
        for x in range(size_x + 1):
            v = ue[0, x]
            s = v + z_up(v)
            q0 = s + y_up(s)
            v = ue[1, x]
            s = v + z_up(v)
            q1 = y_up(s) - s
            v = ue[2, x]
            s = z_up(v) - v
            q2 = s + y_up(s)
            if x:
                value = (q0 - before[0]) + (q1 + before[1]) + (q2 + before[2])
                r = (x - 1) * size_y
                out[r : r + size_y, :] = 0.25 * mask[x - 1].astype(f32) * value[0:size_y]
            before = (q0, q1, q2)

    @pl.when(~at.mech)
    def _():
        high_id, low_id = sub((rows, 128)), sub((128, 128))

        def row(x, y):
            h = host[x, y : y + 1, :]
            left = jnp.where(high_id == (h >> 7), 1.0, 0.0).astype(bf16)
            right = jnp.where(low_id == (h & 127), 1.0, 0.0).astype(bf16)
            return left, right

        out[0:rows, :] = onehot_sum(None, size_x, size_y, (rows, 128), row)
        out[rows : rows + size_y, :] = zmsg[...]


def gather_body(*refs):
    at = Place()
    k = at.groups - 1
    got, refs = refs[:k], refs[k:]
    p, src, sto, well, host = refs[:5]
    tile, xa, xb, ya, yb, xyaa, xyab, xyba, xybb, stiffness = refs[5:15]
    out, out_a, out_b, g0, we, k_high, k_low, ext, acc, table = refs[15:]
    size_x, size_y = p.shape[0], p.shape[1]
    rows = size_x * size_y

    def pick(partner, index):
        value = got[0][index]
        for i in range(1, k):
            value = jnp.where((at.g ^ partner) == i + 1, got[i][index], value)
        return value

    @pl.when(~at.mech)
    def _():
        table[...] = pick(at.groups - 1, (slice(0, rows), slice(None)))
        zrows = (slice(rows, rows + size_y), slice(None))
        before = jnp.where(at.g > 0, pick(at.g - 1, zrows), 0.0)
        after = jnp.where(at.g < at.groups - 2, pick(at.g + 1, zrows), 0.0)
        spot = lane((size_y, 128))
        zside = jnp.where((spot & 7) < 3, before, after)
        first_host = z_slot(3, 0, size_x)
        zhost = jnp.where(spot >= first_host, zside, 0.0).astype(jnp.int32)
        cells = [host[x] for x in range(size_x)] + [zhost]
        cells = [c[8 * t : 8 * t + 8] for c in cells for t in range(size_y // 8)]
        highs = [c >> 7 for c in cells]
        lows = [c & 127 for c in cells]

        def step(h, values):
            line = jnp.broadcast_to(table[pl.ds(h, 1), :], (8, 128))
            return tuple(
                jnp.where(hi == h, jnp.take_along_axis(line, lo, axis=1, mode="promise_in_bounds"), v)
                for hi, lo, v in zip(highs, lows, values)
            )

        values = lax.fori_loop(0, rows, step, tuple(jnp.zeros((8, 128), f32) for _ in cells), unroll=4)
        per = size_y // 8
        strain = [jnp.concatenate(values[per * i : per * i + per], axis=0) for i in range(size_x + 1)]

        def z_tile(field, x, depth, source):
            value = roll(source, -(z_slot(field, x, size_x) + 3), 1)
            return jnp.where((spot < depth) | (spot >= 128 - depth), value, 0.0)

        for x in range(size_x):
            diag = 6.0 + sto[x] + well_index * well[x].astype(f32)
            out[0, x, :, 0:128] = p[x]
            out[0, x, :, 128:256] = z_tile(0, x, 3, zside)
            out[1, x, :, 0:128] = relaxation / diag
            out[1, x, :, 128:256] = z_tile(1, x, 2, zside)
            out[2, x, :, 0:128] = src[x] - biot_coef * strain[x]
            out[2, x, :, 128:256] = z_tile(2, x, 2, zside) - biot_coef * z_tile(3, x, 2, strain[size_x])
        pack_rows(at, out, out_a, out_b, 3, size_x, size_y)

    @pl.when(at.mech)
    def _():
        extend(at, ext, tile, xa, xb, ya, yb, (xyaa, xyab), (xyba, xybb), 7, size_x, size_y)
        we[...] = ext[6]
        spread_stiffness(stiffness, k_high, k_low)
        add_apply(ext, we, acc, k_high, k_low, 1, size_x + 5)
        for m in range(3):
            for x in range(2, size_x + 5):
                g0[m, x] = ext[3 + m, x] - acc[m, x] - spring_coef * ext[m, x]


def flow_body(tile, xa, xb, ya, yb, xyaa, xyab, xyba, xybb, sto, well, block, basis, host, pressure, sums, ext, work, corr):
    at = Place()
    size_x, size_y = sto.shape[0], sto.shape[1]
    rows = size_x * size_y
    nx = size_x + 2 * H

    @pl.when(at.mech)
    def _():
        pressure[...] = jnp.zeros_like(pressure)

    @pl.when(~at.mech)
    def _():
        extend(at, ext, tile, xa, xb, ya, yb, (xyaa, xyab), (xyba, xybb), 3, size_x, size_y)

        def around(field, x):
            v = field[x]
            total = field[x + 1] + field[x - 1]
            total = total + y_up(v) + y_down(v)
            return total + roll(v, 1, 1) + roll(v, -1, 1)

        p0 = [ext[0, x] for x in range(nx)]
        p1 = [None] * nx
        for x in range(1, nx - 1):
            p1[x] = (1.0 - relaxation) * p0[x] + ext[1, x] * (ext[2, x] + around(p0, x))
        p2 = [None] * nx
        for x in range(2, nx - 2):
            p2[x] = (1.0 - relaxation) * p1[x] + ext[1, x] * (ext[2, x] + around(p1, x))
        own = slice(TOP, TOP + size_y)
        for x in range(size_x):
            r = slice(x * size_y, (x + 1) * size_y)
            diag = 6.0 + sto[x] + well_index * well[x].astype(f32)
            here = p2[x + H]
            res = (ext[2, x + H] + around(p2, x + H))[own, 0:128] - diag * here[own, 0:128]
            work[0, r, :] = here[own, 0:128]
            work[1, r, :] = res
            work[2, r, :] = diag
        block_ids = sub((NBLK, 128))

        def coarse_row(x, y):
            r = x * size_y + y
            w = basis[pl.ds(r, 8, stride=rows), :]
            res = work[1, pl.ds(r, 1), :]
            diag = work[2, pl.ds(r, 1), :]
            high, low = split(jnp.concatenate([w * res, w * w * diag], axis=0))
            right = jnp.where(block_ids == block[x, y : y + 1, :], 1.0, 0.0).astype(bf16)
            return jnp.concatenate([high, low], axis=0), right

        acc = onehot_sum(None, size_x, size_y, (32, NBLK), coarse_row)
        corr[...] = jnp.zeros_like(corr)
        corr[:, 0:NBLK] = (acc[0:8] + acc[16:24]) / (1.0 + (acc[8:16] + acc[24:32]))
        lines = [jnp.broadcast_to(corr[j : j + 1, :], (8, 128)) for j in range(8)]
        for x in range(size_x):
            for t in range(size_y // 8):
                ids = block[x, 8 * t : 8 * t + 8, :]
                r = x * size_y + 8 * t
                delta = jnp.zeros((8, 128), f32)
                for j in range(8):
                    got = jnp.take_along_axis(lines[j], ids, axis=1, mode="promise_in_bounds")
                    delta = delta + basis[j * rows + r : j * rows + r + 8, :] * got
                updated = work[0, r : r + 8, :] + delta
                pressure[x, 8 * t : 8 * t + 8, :] = updated
                change = updated - tile[0, x, 8 * t : 8 * t + 8, 0:128]
                high = change.astype(bf16).astype(f32)
                work[0, r : r + 8, :] = high
                work[1, r : r + 8, :] = change - high
        high_id, low_id = sub((rows, 128)), sub((128, 128))

        def sum_row(x, y):
            r = x * size_y + y
            h = host[x, y : y + 1, :]
            hit = high_id == (h >> 7)
            left = [jnp.where(hit, work[i, pl.ds(r, 1), :], 0.0).astype(bf16) for i in range(2)]
            right = jnp.where(low_id == (h & 127), 1.0, 0.0).astype(bf16)
            return jnp.concatenate(left, axis=0), right

        acc = onehot_sum(None, size_x, size_y, (2 * rows, 128), sum_row)
        sums[...] = acc[0:rows] + acc[rows : 2 * rows]


def element_body(*refs):
    at = Place()
    k = at.groups - 1
    sums, counts, refs = refs[:k], refs[k : 2 * k], refs[2 * k :]
    mask, out, out_a, out_b = refs
    size_x, size_y = mask.shape[0], mask.shape[1]

    @pl.when(at.mech)
    def _():
        for x in range(size_x):
            r = slice(x * size_y, (x + 1) * size_y)
            total = sums[0][r, :]
            count = counts[0][r, :]
            for i in range(1, k):
                total = total + sums[i][r, :]
                count = count + counts[i][r, :]
            out[0, x] = mask[x].astype(f32) * (total / jnp.maximum(count, 1.0))
        pack_rows(at, out, out_a, out_b, 1, size_x, size_y)


def krylov_body(tile, xa, xb, ya, yb, xyaa, xyab, xyba, xybb, g0, we, k_high, k_low, r_out, q_out, scal, ext, res, acc):
    at = Place()
    size_x, size_y = tile.shape[1], tile.shape[2]
    rows = ext.shape[2]
    own = slice(TOP, TOP + size_y)

    @pl.when(at.mech)
    def _():
        extend(at, ext, tile, xa, xb, ya, yb, (xyaa, xyab), (xyba, xybb), 1, size_x, size_y)
        line = sub((rows, 128))
        inside = ((line >= TOP) | at.yprev) & ((line < TOP + size_y) | at.ynext)

        def inside_x(x):
            if x < H:
                return inside & at.xprev
            if x >= H + size_x:
                return inside & at.xnext
            return inside

        before = None
        for x in range(1, size_x + 5):
            e = ext[0, x]
            sz = e + z_down(e)
            ssz = sz + y_down(sz)
            dsz = y_down(sz) - sz
            dz = z_down(e) - e
            sdz = dz + y_down(dz)
            if before is not None:
                f = (before[0] - ssz, before[1] + dsz, before[2] + sdz)
                for m in range(3):
                    value = g0[m, x] + (0.25 * biot_coef) * f[m]
                    res[m, x] = jnp.where(inside_x(x), value, 0.0)
            before = (ssz, dsz, sdz)

        add_apply(res, we, acc, k_high, k_low, 2, size_x + 4)
        rr = jnp.zeros((8, 128), f32)
        rq = jnp.zeros((8, 128), f32)
        for m in range(3):
            for x in range(H, H + size_x + 1):
                q = jnp.where(inside_x(x), acc[m, x] + spring_coef * res[m, x], 0.0)
                acc[m, x] = q
                if x < H + size_x:
                    for t in range(TOP, TOP + size_y, 8):
                        v = res[m, x, t : t + 8, :]
                        rr = rr + v * v
                        rq = rq + v * q[t : t + 8]
        rr = total_of(rr)
        shift = total_of(rq) / jnp.maximum(rr, 1e-30)
        rq = jnp.zeros((8, 128), f32)
        qq = jnp.zeros((8, 128), f32)
        for m in range(3):
            for x in range(H, H + size_x + 1):
                q = acc[m, x] - shift * res[m, x]
                acc[m, x] = q
                if x < H + size_x:
                    q_out[m, x - H] = q[own]
                    r_out[m, x - H] = res[m, x, own, :]
                    for t in range(TOP, TOP + size_y, 8):
                        v = q[t : t + 8]
                        qq = qq + v * v
                        rq = rq + v * res[m, x, t : t + 8, :]
        rq, qq = total_of(rq), total_of(qq)
        tiles = range(TOP // 8, (TOP + size_y) // 8)

        def plane(x, sums):
            uq = stack_tiles(corners(acc, x), tiles)
            ur = stack_tiles(corners(res, x), tiles)
            vq = stiff(k_high, k_low, uq)
            vr = stiff(k_high, k_low, ur)
            w = jnp.concatenate([we[x, 8 * t : 8 * t + 8, :] for t in tiles], axis=1)
            out = []
            for s, u, v in zip(sums, (uq, ur, ur), (vq, vq, vr)):
                part = u * v
                t = part[0:8]
                for j in range(1, 24):
                    t = t + part[8 * j : 8 * j + 8]
                out.append(s + w * t)
            return tuple(out)

        zero = jnp.zeros((8, 128 * len(tiles)), f32)
        e11, e12, e22 = lax.fori_loop(H, H + size_x, plane, (zero, zero, zero))
        e11 = total_of(e11) + spring_coef * qq
        e12 = total_of(e12) + spring_coef * rq
        e22 = total_of(e22) + spring_coef * rr
        line = sub((8, 128))
        value = jnp.zeros((8, 128), f32)
        for i, v in enumerate((rr, shift, rq, qq, e11, e12, e22)):
            value = jnp.where(line == i, v, value)
        if scal.shape[0] == 8:
            scal[...] = value
        else:
            scal[0:8] = jnp.where(at.xodd, 0.0, value)
            scal[8:16] = jnp.where(at.xodd, value, 0.0)


def final_body(*refs):
    at = Place()
    scals, own, r, q, u, out = refs[:-5], *refs[-5:]

    @pl.when(~at.mech)
    def _():
        out[...] = jnp.zeros_like(out)

    @pl.when(at.mech)
    def _():
        parts = [s[8 * i : 8 * i + 8] for s in scals for i in range(s.shape[0] // 8)]
        get = lambda part, i: part[i : i + 1]
        total = lambda fn: functools.reduce(lambda a, b: a + b, [fn(p) for p in parts])
        rr = total(lambda p: get(p, 0))
        mean = total(lambda p: get(p, 2) + get(p, 1) * get(p, 0)) / rr

        def shifted(low, mid, high):
            def one(p):
                gap = get(p, 1) - mean
                return get(p, high) + gap * (2.0 * get(p, mid) + gap * get(p, low))

            return total(one)

        qq = shifted(0, 2, 3)
        energy = shifted(6, 5, 4)
        ratio = qq / (mean * mean * rr)
        curve = energy / (mean * mean) - ratio * ratio * mean * rr
        second = ratio * rr / curve
        shift = own[1:2]
        if own.shape[0] == 16:
            shift = jnp.where(at.xodd, own[9:10], shift)
        by_r = 1.0 / mean + second * (ratio - (shift - mean) / mean)
        by_q = -second / mean
        out[...] = u[...] + by_r[None, None] * r[...] + by_q[None, None] * q[...]


def neighbours(tile, msg_a, msg_b):
    xa, xb = both(tile, tile, "gx")
    ya, yb = both(msg_a, msg_b, "gy")
    xyaa, xyba = both(ya, ya, "gx")
    xyab, xybb = both(yb, yb, "gx")
    return (xa, xb, ya, yb, xyaa, xyab, xyba, xybb)


def local(
    pressure,
    source,
    storage,
    well_mask,
    block_id,
    basis_weight,
    host_elem,
    displacement,
    body_force,
    modulus,
    elem_mask,
    stiffness,
):
    p, src, sto, well = pressure[0], source[0], storage[0], well_mask[0]
    host, block, mask = host_elem[0], block_id[0], elem_mask[0]
    size_x, size_y, size_z = p.shape
    rows = size_x * size_y
    basis = basis_weight[0].reshape(8 * rows, size_z)
    u, body = displacement[0], body_force[0]
    nx, ny = size_x + 2 * H, size_y + 2 * TOP
    kron = jax.ShapeDtypeStruct((8 * stiffness.shape[0],) * 2, bf16)

    msg = (7 * size_x * H, size_z)
    tile, ya, yb, zmsg = call(
        pack_body,
        "pack",
        [(7, size_x, size_y, size_z), msg, msg, (size_y, size_z)],
        p, src, sto, well, host, u, body, modulus[0], mask,
    )
    near = neighbours(tile, ya, yb)
    (line,) = call(
        strain_body,
        "strain",
        [(rows + size_y, size_z)],
        tile, *near, mask, host, zmsg,
        scratch=[pltpu.VMEM((3, size_x + 1, size_y + 8, size_z), f32)],
    )
    got = by_xor(line, "grp")
    msg = (3 * size_x * H, 2 * size_z)
    cells, ya, yb, g0, we, k_high, k_low = call(
        gather_body,
        "gather",
        [(3, size_x, size_y, 2 * size_z), msg, msg, (3, nx, ny, size_z), (nx, ny, size_z), kron, kron],
        *got, p, src, sto, well, host, tile, *near, stiffness,
        scratch=[
            pltpu.VMEM((7, nx, ny, size_z), f32),
            pltpu.VMEM((3, nx, ny, size_z), f32),
            pltpu.VMEM((rows, size_z), f32),
        ],
    )
    near = neighbours(cells, ya, yb)
    updated, sums = call(
        flow_body,
        "flow",
        [(size_x, size_y, size_z), (rows, size_z)],
        cells, *near, sto, well, block, basis, host,
        scratch=[
            pltpu.VMEM((3, nx, ny, 2 * size_z), f32),
            pltpu.VMEM((3, rows, size_z), f32),
            pltpu.VMEM((8, size_z), f32),
        ],
    )
    summed = by_xor(sums, "grp")
    msg = (size_x * H, size_z)
    elem, ya, yb = call(
        element_body,
        "element",
        [(1, size_x, size_y, size_z), msg, msg],
        *summed, *got, mask,
    )
    near = neighbours(elem, ya, yb)
    own = (3, size_x, size_y, size_z)
    duo = lax.axis_size("gx") == 2
    r, q, scal = call(
        krylov_body,
        "krylov",
        [own, own, (16 if duo else 8, size_z)],
        elem, *near, g0, we, k_high, k_low,
        scratch=[
            pltpu.VMEM((1, nx, ny, size_z), f32),
            pltpu.VMEM((3, nx, ny, size_z), f32),
            pltpu.VMEM((3, nx, ny, size_z), f32),
        ],
    )
    if duo:
        pair = scal + swap_a(scal, "gx")
        scals = [pair] + by_xor(pair, "gy")
    else:
        scals = [lax.all_gather(scal, ("gx", "gy"), tiled=True)]
    (moved,) = call(final_body, "final", [own], *scals, scal, r, q, u)
    return (updated[None], moved[None])


def solution(mesh):
    cell = P("grp", "gx", "gy", None)
    deep = P("grp", None, "gx", "gy", None)
    placed = (cell, cell, cell, cell, cell, deep, cell, deep, deep, cell, cell, P())
    return jax.shard_map(
        local,
        mesh=mesh,
        in_specs=placed,
        out_specs=(cell, deep),
        check_vma=False,
    )
```

```python
import functools
import jax
import jax.numpy as jnp
from jax import lax
from jax.experimental import pallas as pl
from jax.experimental.pallas import tpu as pltpu
from jax.sharding import PartitionSpec as P

NBLK = 64

biot_coef = 1.5
relaxation = 0.8
spring_coef = 0.5
well_index = 4.0

H = 3
TOP = 8
GRANT = 16 * 1024 * 1024
f32 = jnp.float32
bf16 = jnp.bfloat16


ALL = ("grp", "gx", "gy")


def permuted(value, target):
    sizes = [lax.axis_size(a) for a in ALL]
    flat = lambda g, x, y: (g * sizes[1] + x) * sizes[2] + y
    pairs = []
    for g in range(sizes[0]):
        for x in range(sizes[1]):
            for y in range(sizes[2]):
                pairs.append((flat(g, x, y), flat(*target(g, x, y))))
    return lax.ppermute(value, ALL, pairs)


def idle(g, x, y):
    return g, x ^ 1, y


def x_swap(value):
    return permuted(value, idle)


def exchange_x(value):
    n = lax.axis_size("gx")
    got = x_swap(value)
    if n == 2:
        return got, got
    return got, permuted(value, lambda g, x, y: (g, ((x + 1) if x % 2 else (x - 1)) % n, y))


def up_or_down(i, n, kind):
    j = i + 1 if i % 2 == kind else i - 1
    return j if 0 <= j < n else None


def pair_y(kind):
    n = lax.axis_size("gy")

    def target(g, x, y):
        j = up_or_down(y, n, kind)
        return idle(g, x, y) if j is None else (g, x, j)

    return target


def pair_first(kind):
    last = lax.axis_size("grp") - 1
    along_y = pair_y(kind)

    def target(g, x, y):
        if g == last:
            return along_y(g, x, y)
        j = up_or_down(g, last, kind)
        return idle(g, x, y) if j is None else (j, x, y)

    return target


def star(value):
    n = lax.axis_size("grp")

    def meet(k):
        def target(g, x, y):
            return (g ^ k, x, y) if n - 1 in (g, g ^ k) else idle(g, x, y)

        return target

    return [permuted(value, meet(k)) for k in range(1, n)]


def call(body, name, outs, *args, scratch=(), space=pltpu.VMEM):
    vmem = pl.BlockSpec(memory_space=pltpu.VMEM)
    source = pl.BlockSpec(memory_space=space)
    unique, spots = [], []
    for arg in args:
        found = [i for i, other in enumerate(unique) if other is arg]
        if not found:
            unique.append(arg)
        spots.append(found[0] if found else len(unique) - 1)

    def expanded(*refs):
        return body(*[refs[i] for i in spots], *refs[len(unique) :])

    return pl.pallas_call(
        expanded,
        name=name,
        out_shape=[o if hasattr(o, "dtype") else jax.ShapeDtypeStruct(o, f32) for o in outs],
        in_specs=[source] * len(unique),
        out_specs=[vmem] * len(outs),
        scratch_shapes=list(scratch),
        compiler_params=pltpu.CompilerParams(vmem_limit_bytes=GRANT),
    )(*unique)


class Place:
    def __init__(self):
        self.groups = lax.axis_size("grp")
        self.g = lax.axis_index("grp")
        self.mech = self.g == self.groups - 1
        for name in ("x", "y"):
            n, i = lax.axis_size("g" + name), lax.axis_index("g" + name)
            setattr(self, name + "odd", lax.rem(i, 2) == 1)
            setattr(self, name + "prev", i > 0)
            setattr(self, name + "next", i < n - 1)


def lane(shape):
    return lax.broadcasted_iota(jnp.int32, shape, len(shape) - 1)


def sub(shape):
    return lax.broadcasted_iota(jnp.int32, shape, len(shape) - 2)


def roll(value, shift, axis):
    return pltpu.roll(value, shift % value.shape[axis], axis)


def z_up(value):
    n = value.shape[-1]
    return jnp.where(lane(value.shape) < n - 1, roll(value, -1, value.ndim - 1), 0.0)


def z_down(value):
    return jnp.where(lane(value.shape) > 0, roll(value, 1, value.ndim - 1), 0.0)


def y_up(value):
    return roll(value, -1, value.ndim - 2)


def y_down(value):
    return roll(value, 1, value.ndim - 2)


def pack_rows(at, tile, out_a, out_b, fields, size_x, size_y):
    for f in range(fields):
        for x in range(size_x):
            low = tile[f, x, 0:H, :]
            high = tile[f, x, size_y - H : size_y, :]
            r = (f * size_x + x) * H
            out_a[r : r + H, :] = jnp.where(at.yodd, low, high)
            out_b[r : r + H, :] = jnp.where(at.yodd, high, low)


def extend(at, ext, tile, xa, xb, ya, yb, xya, xyb, fields, size_x, size_y):
    rows = ext.shape[2]
    lanes = ext.shape[3]
    blank_low = jnp.zeros((TOP, lanes), f32)
    blank_high = jnp.zeros((rows - TOP - size_y, lanes), f32)

    def side(valid, odd_is, a, b, index):
        value = jnp.where(odd_is, a[index], b[index])
        return jnp.where(valid, value, 0.0)

    def fill(f, xe, xs, valid, own, msg_a, msg_b):
        ext[f, xe, 0:TOP, :] = blank_low
        ext[f, xe, TOP + size_y : rows, :] = blank_high
        ext[f, xe, TOP : TOP + size_y, :] = own
        r = (f * size_x + xs) * H
        index = (slice(r, r + H), slice(None))
        before = side(valid & at.yprev, at.yodd, msg_a, msg_b, index)
        after = side(valid & at.ynext, ~at.yodd, msg_a, msg_b, index)
        ext[f, xe, TOP - H : TOP, :] = before
        ext[f, xe, TOP + size_y : TOP + size_y + H, :] = after

    class Mixed:
        def __init__(self, pick_a, a, b):
            self.pick_a, self.a, self.b = pick_a, a, b

        def __getitem__(self, index):
            if self.a is self.b:
                return self.a[index]
            return jnp.where(self.pick_a, self.a[index], self.b[index])

    always = at.g >= 0
    for f in range(fields):
        for x in range(size_x):
            fill(f, H + x, x, always, tile[f, x], ya, yb)
        for k in range(H):
            xs = size_x - H + k
            tile_p = Mixed(at.xodd, xa, xb)
            own = jnp.where(at.xprev, tile_p[f, xs], 0.0)
            fill(f, k, xs, at.xprev, own, Mixed(at.xodd, xya[0], xyb[0]), Mixed(at.xodd, xya[1], xyb[1]))
            tile_n = Mixed(~at.xodd, xa, xb)
            own = jnp.where(at.xnext, tile_n[f, k], 0.0)
            fill(f, H + size_x + k, k, at.xnext, own, Mixed(~at.xodd, xya[0], xyb[0]), Mixed(~at.xodd, xya[1], xyb[1]))


def corners(nodes, x):
    out = [None] * 24
    for a in range(2):
        for m in range(3):
            here = nodes[m, x + a]
            up = z_up(here)
            for e, v in ((0, here), (1, up)):
                out[3 * (4 * a + e) + m] = v
                out[3 * (4 * a + 2 + e) + m] = y_up(v)
    return out


def stack_tiles(values, tiles):
    cols = [jnp.concatenate([v[8 * t : 8 * t + 8] for v in values], axis=0) for t in tiles]
    return jnp.concatenate(cols, axis=1)


def split(value):
    high = value.astype(bf16)
    return high, (value - high.astype(f32)).astype(bf16)


def stiff(k_high, k_low, stacked):
    high, low = split(stacked)
    dot = functools.partial(jnp.dot, preferred_element_type=f32)
    return dot(k_high[...], high) + dot(k_high[...], low) + dot(k_low[...], high)


def spread_stiffness(stiffness, k_high, k_low):
    n = 8 * stiffness.shape[0]
    pick = jnp.where(sub((n, n // 8)) // 8 == lane((n, n // 8)), 1.0, 0.0).astype(bf16)
    keep = (sub((n, n)) & 7) == (lane((n, n)) & 7)
    for term, out in zip(split(stiffness[...]), (k_high, k_low)):
        tall = jnp.dot(pick, term, preferred_element_type=f32).astype(bf16)
        wide = lax.dot_general(tall, pick, (((1,), (1,)), ((), ())), preferred_element_type=f32)
        out[...] = jnp.where(keep, wide, 0.0).astype(bf16)


def add_apply(nodes, weight, out, k_high, k_low, first, last, own=None):
    rows = nodes.shape[2]
    tiles = rows // 8
    for m in range(3):
        out[m, first] = jnp.zeros((rows, 128), f32)

    def plane(x, energy):
        u = stack_tiles(corners(nodes, x), range(tiles))
        v = stiff(k_high, k_low, u)
        w = weight[x]

        def entry(j):
            return w * jnp.concatenate(
                [v[8 * j : 8 * j + 8, 128 * t : 128 * t + 128] for t in range(tiles)], axis=0
            )

        for a in range(2):
            for m in range(3):
                part = []
                for b in range(2):
                    c = 4 * a + 2 * b
                    part.append(entry(3 * c + m) + z_down(entry(3 * (c + 1) + m)))
                total = part[0] + y_down(part[1])
                if a == 0:
                    out[m, x] = out[m, x] + total
                else:
                    out[m, x + 1] = total
        if own is None:
            return energy
        planes, spots = own
        inside = jnp.where((x >= planes[0]) & (x < planes[-1] + 1), 1.0, 0.0)
        for t in spots:
            cols = slice(128 * t, 128 * t + 128)
            energy = energy + inside * w[8 * t : 8 * t + 8] * dots(u[:, cols], v[:, cols])
        return energy

    return lax.fori_loop(first, last, plane, jnp.zeros((8, 128), f32))


def dots(u, v):
    part = u * v
    total = part[0:8]
    for j in range(1, 24):
        total = total + part[8 * j : 8 * j + 8]
    return total


def total_of(value):
    return jnp.sum(jnp.sum(value, axis=0, keepdims=True), axis=1, keepdims=True)


def onehot_sum(size_x, size_y, shape, row_fn):
    def plane(x, acc):
        lefts, rights = [], []
        for y in range(size_y):
            left, right = row_fn(x, y)
            lefts.append(left)
            rights.append(right)
        return acc + lax.dot_general(
            jnp.concatenate(lefts, axis=1),
            jnp.concatenate(rights, axis=1),
            (((1,), (1,)), ((), ())),
            preferred_element_type=f32,
        )

    return lax.fori_loop(0, size_x, plane, jnp.zeros(shape, f32))


def z_slot(field, x, size_x):
    return 8 * (field * size_x + x)


def pack_body(p, src, sto, well, host, u, body, mod, mask, tile, ya, yb, *scratch):
    at = Place()
    size_x, size_y = p.shape[0], p.shape[1]
    refs, sems = scratch[:-1], scratch[-1]

    def fetch(first, sources):
        copies = [
            pltpu.make_async_copy(s, refs[first + i], sems.at[first + i])
            for i, s in enumerate(sources)
        ]
        for c in copies:
            c.start()
        for c in copies:
            c.wait()
        return refs[first : first + len(copies)]

    @pl.when(at.mech)
    def _():
        u_in, body_in, mod_in, mask_in = fetch(0, (u, body, mod, mask))
        tile[0:3] = u_in[...]
        tile[3:6] = body_in[...]
        tile[6] = mod_in[...] * mask_in[...].astype(f32)
        pack_rows(at, tile, ya, yb, 7, size_x, size_y)

    @pl.when(~at.mech)
    def _():
        p_in, src_in, sto_in, well_in, host_in = fetch(4, (p, src, sto, well, host))
        where = lane((size_y, 128))
        msg = jnp.zeros((size_y, 128), f32)
        for x in range(size_x):
            diag = 6.0 + sto_in[x] + well_index * well_in[x].astype(f32)
            fields = (p_in[x], relaxation / diag, src_in[x], host_in[x].astype(f32))
            for f, v in enumerate(fields):
                s = z_slot(f, x, size_x)
                msg = jnp.where((where >= s) & (where < s + 6), roll(v, s + 3, 1), msg)
        ya[0:size_y] = msg
        yb[0:size_y] = msg


def count_body(host, out):
    at = Place()
    size_x, size_y = host.shape[0], host.shape[1]
    rows = size_x * size_y

    @pl.when(~at.mech)
    def _():
        high_id, low_id = sub((rows, 128)), sub((128, 128))

        def row(x, y):
            h = host[x, y : y + 1, :]
            left = jnp.where(high_id == (h >> 7), 1.0, 0.0).astype(bf16)
            right = jnp.where(low_id == (h & 127), 1.0, 0.0).astype(bf16)
            return left, right

        out[...] = onehot_sum(size_x, size_y, (rows, 128), row)


def strain_body(tile, xa, xb, ya, yb, xyaa, xyab, xyba, xybb, mask, counts, out, ue):
    at = Place()
    size_x, size_y = mask.shape[0], mask.shape[1]

    @pl.when(at.mech)
    def _():
        for m in range(3):
            for x in range(size_x + 1):
                r = (m * size_x + (x if x < size_x else 0)) * H
                if x < size_x:
                    own = tile[m, x]
                    after = jnp.where(at.yodd, yb[r : r + 1, :], ya[r : r + 1, :])
                else:
                    own = jnp.where(at.xodd, xb[m, 0], xa[m, 0])
                    of_a = jnp.where(at.yodd, xyab[r : r + 1, :], xyaa[r : r + 1, :])
                    of_b = jnp.where(at.yodd, xybb[r : r + 1, :], xyba[r : r + 1, :])
                    after = jnp.where(at.xodd, of_b, of_a)
                    own = jnp.where(at.xnext, own, 0.0)
                    after = jnp.where(at.xnext, after, 0.0)
                ue[m, x, 0:size_y, :] = own
                ue[m, x, size_y : size_y + 8, :] = jnp.zeros((8, 128), f32)
                ue[m, x, size_y : size_y + 1, :] = jnp.where(at.ynext, after, 0.0)
        before = None
        for x in range(size_x + 1):
            v = ue[0, x]
            s = v + z_up(v)
            q0 = s + y_up(s)
            v = ue[1, x]
            s = v + z_up(v)
            q1 = y_up(s) - s
            v = ue[2, x]
            s = z_up(v) - v
            q2 = s + y_up(s)
            if x:
                value = (q0 - before[0]) + (q1 + before[1]) + (q2 + before[2])
                r = (x - 1) * size_y
                out[r : r + size_y, :] = 0.25 * mask[x - 1].astype(f32) * value[0:size_y]
            before = (q0, q1, q2)

    @pl.when(~at.mech)
    def _():
        out[...] = counts[...]


def gather_body(*refs):
    at = Place()
    k = at.groups - 1
    got, refs = refs[:k], refs[k:]
    p, src, sto, well, host = refs[:5]
    tile, xa, xb, ya, yb, xyaa, xyab, xyba, xybb, stiffness = refs[5:15]
    out, out_a, out_b, g0, we, k_high, k_low, ext, acc, table = refs[15:]
    size_x, size_y = p.shape[0], p.shape[1]
    rows = size_x * size_y

    def pick(partner, index):
        value = got[0][index]
        for i in range(1, k):
            value = jnp.where((at.g ^ partner) == i + 1, got[i][index], value)
        return value

    @pl.when(~at.mech)
    def _():
        table[...] = pick(at.groups - 1, slice(None))
        godd = lax.rem(at.g, 2) == 1
        msg_a, msg_b = ya[0:size_y], yb[0:size_y]
        before = jnp.where(at.g > 0, jnp.where(godd, msg_a, msg_b), 0.0)
        after = jnp.where(at.g < at.groups - 2, jnp.where(godd, msg_b, msg_a), 0.0)
        spot = lane((size_y, 128))
        zside = jnp.where((spot & 7) < 3, before, after)
        first_host = z_slot(3, 0, size_x)
        zhost = jnp.where(spot >= first_host, zside, 0.0).astype(jnp.int32)
        cells = [host[x] for x in range(size_x)] + [zhost]
        cells = [c[8 * t : 8 * t + 8] for c in cells for t in range(size_y // 8)]
        highs = [c >> 7 for c in cells]
        lows = [c & 127 for c in cells]

        def step(h, values):
            line = jnp.broadcast_to(table[pl.ds(h, 1), :], (8, 128))
            return tuple(
                jnp.where(hi == h, jnp.take_along_axis(line, lo, axis=1, mode="promise_in_bounds"), v)
                for hi, lo, v in zip(highs, lows, values)
            )

        values = lax.fori_loop(0, rows, step, tuple(jnp.zeros((8, 128), f32) for _ in cells), unroll=4)
        per = size_y // 8
        strain = [jnp.concatenate(values[per * i : per * i + per], axis=0) for i in range(size_x + 1)]

        def z_tile(field, x, depth, source):
            value = roll(source, -(z_slot(field, x, size_x) + 3), 1)
            return jnp.where((spot < depth) | (spot >= 128 - depth), value, 0.0)

        for x in range(size_x):
            diag = 6.0 + sto[x] + well_index * well[x].astype(f32)
            out[0, x, :, 0:128] = p[x]
            out[0, x, :, 128:256] = z_tile(0, x, 3, zside)
            out[1, x, :, 0:128] = relaxation / diag
            out[1, x, :, 128:256] = z_tile(1, x, 2, zside)
            out[2, x, :, 0:128] = src[x] - biot_coef * strain[x]
            out[2, x, :, 128:256] = z_tile(2, x, 2, zside) - biot_coef * z_tile(3, x, 2, strain[size_x])
        pack_rows(at, out, out_a, out_b, 3, size_x, size_y)

    @pl.when(at.mech)
    def _():
        extend(at, ext, tile, xa, xb, ya, yb, (xyaa, xyab), (xyba, xybb), 7, size_x, size_y)
        we[...] = ext[6]
        spread_stiffness(stiffness, k_high, k_low)
        add_apply(ext, we, acc, k_high, k_low, 1, size_x + 5)
        for m in range(3):
            for x in range(2, size_x + 5):
                g0[m, x] = ext[3 + m, x] - acc[m, x] - spring_coef * ext[m, x]


def flow_body(tile, xa, xb, ya, yb, xyaa, xyab, xyba, xybb, sto, well, block, basis, host, pressure, sums, ext, work, corr):
    at = Place()
    size_x, size_y = sto.shape[0], sto.shape[1]
    rows = size_x * size_y
    nx = size_x + 2 * H

    @pl.when(~at.mech)
    def _():
        extend(at, ext, tile, xa, xb, ya, yb, (xyaa, xyab), (xyba, xybb), 3, size_x, size_y)

        def around(field, x):
            v = field[x]
            total = field[x + 1] + field[x - 1]
            total = total + y_up(v) + y_down(v)
            return total + roll(v, 1, 1) + roll(v, -1, 1)

        p0 = [ext[0, x] for x in range(nx)]
        p1 = [None] * nx
        for x in range(1, nx - 1):
            p1[x] = (1.0 - relaxation) * p0[x] + ext[1, x] * (ext[2, x] + around(p0, x))
        p2 = [None] * nx
        for x in range(2, nx - 2):
            p2[x] = (1.0 - relaxation) * p1[x] + ext[1, x] * (ext[2, x] + around(p1, x))
        own = slice(TOP, TOP + size_y)
        for x in range(size_x):
            r = slice(x * size_y, (x + 1) * size_y)
            diag = 6.0 + sto[x] + well_index * well[x].astype(f32)
            here = p2[x + H]
            res = (ext[2, x + H] + around(p2, x + H))[own, 0:128] - diag * here[own, 0:128]
            work[0, r, :] = here[own, 0:128]
            work[1, r, :] = res
            work[2, r, :] = diag
        block_ids = sub((NBLK, 128))

        def coarse_row(x, y):
            r = x * size_y + y
            w = basis[pl.ds(r, 8, stride=rows), :]
            res = work[1, pl.ds(r, 1), :]
            diag = work[2, pl.ds(r, 1), :]
            high, low = split(jnp.concatenate([w * res, w * w * diag], axis=0))
            right = jnp.where(block_ids == block[x, y : y + 1, :], 1.0, 0.0).astype(bf16)
            return jnp.concatenate([high, low], axis=0), right

        acc = onehot_sum(size_x, size_y, (32, NBLK), coarse_row)
        corr[...] = jnp.zeros_like(corr)
        corr[:, 0:NBLK] = (acc[0:8] + acc[16:24]) / (1.0 + (acc[8:16] + acc[24:32]))
        lines = [jnp.broadcast_to(corr[j : j + 1, :], (8, 128)) for j in range(8)]
        for x in range(size_x):
            for t in range(size_y // 8):
                ids = block[x, 8 * t : 8 * t + 8, :]
                r = x * size_y + 8 * t
                delta = jnp.zeros((8, 128), f32)
                for j in range(8):
                    got = jnp.take_along_axis(lines[j], ids, axis=1, mode="promise_in_bounds")
                    delta = delta + basis[j * rows + r : j * rows + r + 8, :] * got
                updated = work[0, r : r + 8, :] + delta
                pressure[x, 8 * t : 8 * t + 8, :] = updated
                change = updated - tile[0, x, 8 * t : 8 * t + 8, 0:128]
                high = change.astype(bf16).astype(f32)
                work[0, r : r + 8, :] = high
                work[1, r : r + 8, :] = change - high
        high_id, low_id = sub((rows, 128)), sub((128, 128))

        def sum_row(x, y):
            r = x * size_y + y
            h = host[x, y : y + 1, :]
            hit = high_id == (h >> 7)
            left = [jnp.where(hit, work[i, pl.ds(r, 1), :], 0.0).astype(bf16) for i in range(2)]
            right = jnp.where(low_id == (h & 127), 1.0, 0.0).astype(bf16)
            return jnp.concatenate(left, axis=0), right

        acc = onehot_sum(size_x, size_y, (2 * rows, 128), sum_row)
        sums[...] = acc[0:rows] + acc[rows : 2 * rows]


def element_body(*refs):
    at = Place()
    k = at.groups - 1
    sums, counts, refs = refs[:k], refs[k : 2 * k], refs[2 * k :]
    mask, out, out_a, out_b = refs
    size_x, size_y = mask.shape[0], mask.shape[1]

    @pl.when(at.mech)
    def _():
        for x in range(size_x):
            r = slice(x * size_y, (x + 1) * size_y)
            total = sums[0][r, :]
            count = counts[0][r, :]
            for i in range(1, k):
                total = total + sums[i][r, :]
                count = count + counts[i][r, :]
            out[0, x] = mask[x].astype(f32) * (total / jnp.maximum(count, 1.0))
        pack_rows(at, out, out_a, out_b, 1, size_x, size_y)


def krylov_body(tile, xa, xb, ya, yb, xyaa, xyab, xyba, xybb, g0, we, k_high, k_low, r_out, q_out, scal, ext, res, acc):
    at = Place()
    size_x, size_y = tile.shape[1], tile.shape[2]
    rows = ext.shape[2]
    own = slice(TOP, TOP + size_y)

    @pl.when(at.mech)
    def _():
        extend(at, ext, tile, xa, xb, ya, yb, (xyaa, xyab), (xyba, xybb), 1, size_x, size_y)
        line = sub((rows, 128))
        inside = ((line >= TOP) | at.yprev) & ((line < TOP + size_y) | at.ynext)

        def inside_x(x):
            if x < H:
                return inside & at.xprev
            if x >= H + size_x:
                return inside & at.xnext
            return inside

        before = None
        for x in range(1, size_x + 5):
            e = ext[0, x]
            sz = e + z_down(e)
            ssz = sz + y_down(sz)
            dsz = y_down(sz) - sz
            dz = z_down(e) - e
            sdz = dz + y_down(dz)
            if before is not None:
                f = (before[0] - ssz, before[1] + dsz, before[2] + sdz)
                for m in range(3):
                    value = g0[m, x] + (0.25 * biot_coef) * f[m]
                    res[m, x] = jnp.where(inside_x(x), value, 0.0)
            before = (ssz, dsz, sdz)

        tiles = range(TOP // 8, (TOP + size_y) // 8)
        planes = range(H, H + size_x)
        e22 = add_apply(res, we, acc, k_high, k_low, 2, size_x + 4, (planes, tiles))
        rr = jnp.zeros((8, 128), f32)
        rq = jnp.zeros((8, 128), f32)
        for m in range(3):
            for x in range(H, H + size_x + 1):
                q = jnp.where(inside_x(x), acc[m, x] + spring_coef * res[m, x], 0.0)
                acc[m, x] = q
                if x < H + size_x:
                    for t in range(TOP, TOP + size_y, 8):
                        v = res[m, x, t : t + 8, :]
                        rr = rr + v * v
                        rq = rq + v * q[t : t + 8]
        rr = total_of(rr)
        shift = total_of(rq) / jnp.maximum(rr, 1e-30)
        rq = jnp.zeros((8, 128), f32)
        qq = jnp.zeros((8, 128), f32)
        for m in range(3):
            for x in range(H, H + size_x + 1):
                q = acc[m, x] - shift * res[m, x]
                acc[m, x] = q
                if x < H + size_x:
                    q_out[m, x - H] = q[own]
                    r_out[m, x - H] = res[m, x, own, :]
                    for t in range(TOP, TOP + size_y, 8):
                        v = q[t : t + 8]
                        qq = qq + v * v
                        rq = rq + v * res[m, x, t : t + 8, :]
        rq, qq = total_of(rq), total_of(qq)

        def plane(x, sums):
            uq = stack_tiles(corners(acc, x), tiles)
            ur = stack_tiles(corners(res, x), tiles)
            vq = stiff(k_high, k_low, uq)
            w = jnp.concatenate([we[x, 8 * t : 8 * t + 8, :] for t in tiles], axis=1)
            return tuple(s + w * dots(u, vq) for s, u in zip(sums, (uq, ur)))

        zero = jnp.zeros((8, 128 * len(tiles)), f32)
        e11, e12 = lax.fori_loop(H, H + size_x, plane, (zero, zero))
        e11 = total_of(e11) + spring_coef * qq
        e12 = total_of(e12) + spring_coef * rq
        e22 = total_of(e22) + spring_coef * rr
        line = sub((8, 128))
        value = jnp.zeros((8, 128), f32)
        for i, v in enumerate((rr, shift, rq, qq, e11, e12, e22)):
            value = jnp.where(line == i, v, value)
        if scal.shape[0] == 8:
            scal[...] = value
        else:
            scal[0:8] = jnp.where(at.xodd, 0.0, value)
            scal[8:16] = jnp.where(at.xodd, value, 0.0)


def final_body(*refs):
    at = Place()
    scals, own, r, q, u, updated, pressure, out = refs[:-7], *refs[-7:]

    @pl.when(~at.mech)
    def _():
        out[...] = jnp.zeros_like(out)
        pressure[...] = updated[...]

    @pl.when(at.mech)
    def _():
        pressure[...] = jnp.zeros_like(pressure)
        parts = [s[8 * i : 8 * i + 8] for s in scals for i in range(s.shape[0] // 8)]
        get = lambda part, i: part[i : i + 1]
        total = lambda fn: functools.reduce(lambda a, b: a + b, [fn(p) for p in parts])
        rr = total(lambda p: get(p, 0))
        mean = total(lambda p: get(p, 2) + get(p, 1) * get(p, 0)) / rr

        def shifted(low, mid, high):
            def one(p):
                gap = get(p, 1) - mean
                return get(p, high) + gap * (2.0 * get(p, mid) + gap * get(p, low))

            return total(one)

        qq = shifted(0, 2, 3)
        energy = shifted(6, 5, 4)
        ratio = qq / (mean * mean * rr)
        curve = energy / (mean * mean) - ratio * ratio * mean * rr
        second = ratio * rr / curve
        shift = own[1:2]
        if own.shape[0] == 16:
            shift = jnp.where(at.xodd, own[9:10], shift)
        by_r = 1.0 / mean + second * (ratio - (shift - mean) / mean)
        by_q = -second / mean
        out[...] = u[...] + by_r[None, None] * r[...] + by_q[None, None] * q[...]


def neighbours(tile, msg_a, msg_b, pair=pair_y):
    xa, xb = exchange_x(tile)
    yb = permuted(msg_b, pair(1))
    ya = permuted(msg_a, pair(0))
    xyab, xybb = exchange_x(yb)
    xyaa, xyba = exchange_x(ya)
    return (xa, xb, ya, yb, xyaa, xyab, xyba, xybb)


def local(
    pressure,
    source,
    storage,
    well_mask,
    block_id,
    basis_weight,
    host_elem,
    displacement,
    body_force,
    modulus,
    elem_mask,
    stiffness,
):
    p, src, sto, well = pressure[0], source[0], storage[0], well_mask[0]
    host, block, mask = host_elem[0], block_id[0], elem_mask[0]
    size_x, size_y, size_z = p.shape
    rows = size_x * size_y
    basis = basis_weight[0].reshape(8 * rows, size_z)
    u, body = displacement[0], body_force[0]
    nx, ny = size_x + 2 * H, size_y + 2 * TOP
    kron = jax.ShapeDtypeStruct((8 * stiffness.shape[0],) * 2, bf16)

    msg = (7 * size_x * H, size_z)
    inputs = (displacement[0], body_force[0], modulus[0], mask, p, src, sto, well, host)
    tile, ya, yb = call(
        pack_body,
        "pack",
        [(7, size_x, size_y, size_z), msg, msg],
        p, src, sto, well, host, u, body, modulus[0], mask,
        scratch=[pltpu.VMEM(v.shape, v.dtype) for v in inputs]
        + [pltpu.SemaphoreType.DMA((len(inputs),))],
        space=pltpu.HBM,
    )
    near = neighbours(tile, ya, yb, pair_first)
    (counts,) = call(count_body, "count", [(rows, size_z)], host)
    (line,) = call(
        strain_body,
        "strain",
        [(rows, size_z)],
        tile, *near, mask, counts,
        scratch=[pltpu.VMEM((3, size_x + 1, size_y + 8, size_z), f32)],
    )
    got = star(line)
    msg = (3 * size_x * H, 2 * size_z)
    cells, ya, yb, g0, we, k_high, k_low = call(
        gather_body,
        "gather",
        [(3, size_x, size_y, 2 * size_z), msg, msg, (3, nx, ny, size_z), (nx, ny, size_z), kron, kron],
        *got, p, src, sto, well, host, tile, *near, stiffness,
        scratch=[
            pltpu.VMEM((7, nx, ny, size_z), f32),
            pltpu.VMEM((3, nx, ny, size_z), f32),
            pltpu.VMEM((rows, size_z), f32),
        ],
    )
    near = neighbours(cells, ya, yb)
    updated, sums = call(
        flow_body,
        "flow",
        [(size_x, size_y, size_z), (rows, size_z)],
        cells, *near, sto, well, block, basis, host,
        scratch=[
            pltpu.VMEM((3, nx, ny, 2 * size_z), f32),
            pltpu.VMEM((3, rows, size_z), f32),
            pltpu.VMEM((8, size_z), f32),
        ],
    )
    summed = star(sums)
    msg = (size_x * H, size_z)
    elem, ya, yb = call(
        element_body,
        "element",
        [(1, size_x, size_y, size_z), msg, msg],
        *summed, *got, mask,
    )
    near = neighbours(elem, ya, yb)
    own = (3, size_x, size_y, size_z)
    duo = lax.axis_size("gx") == 2
    r, q, scal = call(
        krylov_body,
        "krylov",
        [own, own, (16 if duo else 8, size_z)],
        elem, *near, g0, we, k_high, k_low,
        scratch=[
            pltpu.VMEM((1, nx, ny, size_z), f32),
            pltpu.VMEM((3, nx, ny, size_z), f32),
            pltpu.VMEM((3, nx, ny, size_z), f32),
        ],
    )
    if duo:
        pair = scal + x_swap(scal)
        n = lax.axis_size("gy")
        scals = [pair] + [permuted(pair, lambda g, x, y: (g, x, y ^ k)) for k in range(1, n)]
    else:
        scals = [lax.all_gather(scal, ("gx", "gy"), tiled=True)]
    pressure_out, moved = call(
        final_body, "final", [p.shape, own], *scals, scal, r, q, u, updated
    )
    return (pressure_out[None], moved[None])


def solution(mesh):
    cell = P("grp", "gx", "gy", None)
    deep = P("grp", None, "gx", "gy", None)
    placed = (cell, cell, cell, cell, cell, deep, cell, deep, deep, cell, cell, P())
    return jax.shard_map(
        local,
        mesh=mesh,
        in_specs=placed,
        out_specs=(cell, deep),
        check_vma=False,
    )
```

```python
import functools
import jax
import jax.numpy as jnp
from jax import lax
from jax.experimental import pallas as pl
from jax.experimental.pallas import tpu as pltpu
from jax.sharding import PartitionSpec as P

NBLK = 64

biot_coef = 1.5
relaxation = 0.8
spring_coef = 0.5
well_index = 4.0

H = 3
TOP = 8
GRANT = 16 * 1024 * 1024
f32 = jnp.float32
bf16 = jnp.bfloat16


ALL = ("grp", "gx", "gy")


def permuted(value, target):
    sizes = [lax.axis_size(a) for a in ALL]
    flat = lambda g, x, y: (g * sizes[1] + x) * sizes[2] + y
    pairs = []
    for g in range(sizes[0]):
        for x in range(sizes[1]):
            for y in range(sizes[2]):
                pairs.append((flat(g, x, y), flat(*target(g, x, y))))
    return lax.ppermute(value, ALL, pairs)


def idle(g, x, y):
    return g, x ^ 1, y


def x_swap(value):
    return permuted(value, idle)


def exchange_x(value):
    n = lax.axis_size("gx")
    got = x_swap(value)
    if n == 2:
        return got, got
    return got, permuted(value, lambda g, x, y: (g, ((x + 1) if x % 2 else (x - 1)) % n, y))


def up_or_down(i, n, kind):
    j = i + 1 if i % 2 == kind else i - 1
    return j if 0 <= j < n else None


def pair_y(kind):
    n = lax.axis_size("gy")

    def target(g, x, y):
        j = up_or_down(y, n, kind)
        return idle(g, x, y) if j is None else (g, x, j)

    return target


def pair_first(kind):
    last = lax.axis_size("grp") - 1
    along_y = pair_y(kind)

    def target(g, x, y):
        if g == last:
            return along_y(g, x, y)
        j = up_or_down(g, last, kind)
        return idle(g, x, y) if j is None else (j, x, y)

    return target


def star(value):
    n = lax.axis_size("grp")

    def meet(k):
        def target(g, x, y):
            return (g ^ k, x, y) if n - 1 in (g, g ^ k) else idle(g, x, y)

        return target

    return [permuted(value, meet(k)) for k in range(1, n)]


def call(body, name, outs, *args, scratch=(), space=pltpu.VMEM):
    vmem = pl.BlockSpec(memory_space=pltpu.VMEM)
    source = pl.BlockSpec(memory_space=space)
    unique, spots = [], []
    for arg in args:
        found = [i for i, other in enumerate(unique) if other is arg]
        if not found:
            unique.append(arg)
        spots.append(found[0] if found else len(unique) - 1)

    def expanded(*refs):
        return body(*[refs[i] for i in spots], *refs[len(unique) :])

    if space is pltpu.HBM:
        unique = [pltpu.with_memory_space_constraint(v, space) for v in unique]
    return pl.pallas_call(
        expanded,
        name=name,
        out_shape=[o if hasattr(o, "dtype") else jax.ShapeDtypeStruct(o, f32) for o in outs],
        in_specs=[source] * len(unique),
        out_specs=[vmem] * len(outs),
        scratch_shapes=list(scratch),
        compiler_params=pltpu.CompilerParams(vmem_limit_bytes=GRANT),
    )(*unique)


class Place:
    def __init__(self):
        self.groups = lax.axis_size("grp")
        self.g = lax.axis_index("grp")
        self.mech = self.g == self.groups - 1
        for name in ("x", "y"):
            n, i = lax.axis_size("g" + name), lax.axis_index("g" + name)
            setattr(self, name + "odd", lax.rem(i, 2) == 1)
            setattr(self, name + "prev", i > 0)
            setattr(self, name + "next", i < n - 1)


def lane(shape):
    return lax.broadcasted_iota(jnp.int32, shape, len(shape) - 1)


def sub(shape):
    return lax.broadcasted_iota(jnp.int32, shape, len(shape) - 2)


def roll(value, shift, axis):
    return pltpu.roll(value, shift % value.shape[axis], axis)


def z_up(value):
    n = value.shape[-1]
    return jnp.where(lane(value.shape) < n - 1, roll(value, -1, value.ndim - 1), 0.0)


def z_down(value):
    return jnp.where(lane(value.shape) > 0, roll(value, 1, value.ndim - 1), 0.0)


def y_up(value):
    return roll(value, -1, value.ndim - 2)


def y_down(value):
    return roll(value, 1, value.ndim - 2)


def pack_rows(at, tile, out_a, out_b, fields, size_x, size_y):
    for f in range(fields):
        for x in range(size_x):
            low = tile[f, x, 0:H, :]
            high = tile[f, x, size_y - H : size_y, :]
            r = (f * size_x + x) * H
            out_a[r : r + H, :] = jnp.where(at.yodd, low, high)
            out_b[r : r + H, :] = jnp.where(at.yodd, high, low)


def extend(at, ext, tile, xa, xb, ya, yb, xya, xyb, fields, size_x, size_y):
    rows = ext.shape[2]
    lanes = ext.shape[3]
    blank_low = jnp.zeros((TOP, lanes), f32)
    blank_high = jnp.zeros((rows - TOP - size_y, lanes), f32)

    def side(valid, odd_is, a, b, index):
        value = jnp.where(odd_is, a[index], b[index])
        return jnp.where(valid, value, 0.0)

    def fill(f, xe, xs, valid, own, msg_a, msg_b):
        ext[f, xe, 0:TOP, :] = blank_low
        ext[f, xe, TOP + size_y : rows, :] = blank_high
        ext[f, xe, TOP : TOP + size_y, :] = own
        r = (f * size_x + xs) * H
        index = (slice(r, r + H), slice(None))
        before = side(valid & at.yprev, at.yodd, msg_a, msg_b, index)
        after = side(valid & at.ynext, ~at.yodd, msg_a, msg_b, index)
        ext[f, xe, TOP - H : TOP, :] = before
        ext[f, xe, TOP + size_y : TOP + size_y + H, :] = after

    class Mixed:
        def __init__(self, pick_a, a, b):
            self.pick_a, self.a, self.b = pick_a, a, b

        def __getitem__(self, index):
            if self.a is self.b:
                return self.a[index]
            return jnp.where(self.pick_a, self.a[index], self.b[index])

    always = at.g >= 0
    for f in range(fields):
        for x in range(size_x):
            fill(f, H + x, x, always, tile[f, x], ya, yb)
        for k in range(H):
            xs = size_x - H + k
            tile_p = Mixed(at.xodd, xa, xb)
            own = jnp.where(at.xprev, tile_p[f, xs], 0.0)
            fill(f, k, xs, at.xprev, own, Mixed(at.xodd, xya[0], xyb[0]), Mixed(at.xodd, xya[1], xyb[1]))
            tile_n = Mixed(~at.xodd, xa, xb)
            own = jnp.where(at.xnext, tile_n[f, k], 0.0)
            fill(f, H + size_x + k, k, at.xnext, own, Mixed(~at.xodd, xya[0], xyb[0]), Mixed(~at.xodd, xya[1], xyb[1]))


def corners(nodes, x):
    out = [None] * 24
    for a in range(2):
        for m in range(3):
            here = nodes[m, x + a]
            up = z_up(here)
            for e, v in ((0, here), (1, up)):
                out[3 * (4 * a + e) + m] = v
                out[3 * (4 * a + 2 + e) + m] = y_up(v)
    return out


def stack_tiles(values, tiles):
    cols = [jnp.concatenate([v[8 * t : 8 * t + 8] for v in values], axis=0) for t in tiles]
    return jnp.concatenate(cols, axis=1)


def split(value):
    high = value.astype(bf16)
    return high, (value - high.astype(f32)).astype(bf16)


def stiff(k_high, k_low, stacked):
    high, low = split(stacked)
    dot = functools.partial(jnp.dot, preferred_element_type=f32)
    return dot(k_high[...], high) + dot(k_high[...], low) + dot(k_low[...], high)


def spread_stiffness(stiffness, k_high, k_low):
    n = 8 * stiffness.shape[0]
    pick = jnp.where(sub((n, n // 8)) // 8 == lane((n, n // 8)), 1.0, 0.0).astype(bf16)
    keep = (sub((n, n)) & 7) == (lane((n, n)) & 7)
    for term, out in zip(split(stiffness[...]), (k_high, k_low)):
        tall = jnp.dot(pick, term, preferred_element_type=f32).astype(bf16)
        wide = lax.dot_general(tall, pick, (((1,), (1,)), ((), ())), preferred_element_type=f32)
        out[...] = jnp.where(keep, wide, 0.0).astype(bf16)


def add_apply(nodes, weight, out, k_high, k_low, first, last, own=None):
    rows = nodes.shape[2]
    tiles = rows // 8
    for m in range(3):
        out[m, first] = jnp.zeros((rows, 128), f32)

    def plane(x, energy):
        u = stack_tiles(corners(nodes, x), range(tiles))
        v = stiff(k_high, k_low, u)
        w = weight[x]

        def entry(j):
            return w * jnp.concatenate(
                [v[8 * j : 8 * j + 8, 128 * t : 128 * t + 128] for t in range(tiles)], axis=0
            )

        for a in range(2):
            for m in range(3):
                part = []
                for b in range(2):
                    c = 4 * a + 2 * b
                    part.append(entry(3 * c + m) + z_down(entry(3 * (c + 1) + m)))
                total = part[0] + y_down(part[1])
                if a == 0:
                    out[m, x] = out[m, x] + total
                else:
                    out[m, x + 1] = total
        if own is None:
            return energy
        planes, spots = own
        inside = jnp.where((x >= planes[0]) & (x < planes[-1] + 1), 1.0, 0.0)
        for t in spots:
            cols = slice(128 * t, 128 * t + 128)
            energy = energy + inside * w[8 * t : 8 * t + 8] * dots(u[:, cols], v[:, cols])
        return energy

    return lax.fori_loop(first, last, plane, jnp.zeros((8, 128), f32))


def dots(u, v):
    part = u * v
    total = part[0:8]
    for j in range(1, 24):
        total = total + part[8 * j : 8 * j + 8]
    return total


def total_of(value):
    return jnp.sum(jnp.sum(value, axis=0, keepdims=True), axis=1, keepdims=True)


def onehot_sum(size_x, size_y, shape, row_fn):
    def plane(x, acc):
        lefts, rights = [], []
        for y in range(size_y):
            left, right = row_fn(x, y)
            lefts.append(left)
            rights.append(right)
        return acc + lax.dot_general(
            jnp.concatenate(lefts, axis=1),
            jnp.concatenate(rights, axis=1),
            (((1,), (1,)), ((), ())),
            preferred_element_type=f32,
        )

    return lax.fori_loop(0, size_x, plane, jnp.zeros(shape, f32))


def z_slot(field, x, size_x):
    return 8 * (field * size_x + x)


def pack_body(p, src, sto, well, host, u, body, mod, mask, tile, ya, yb, *scratch):
    at = Place()
    size_x, size_y = p.shape[0], p.shape[1]
    refs, sems = scratch[:-1], scratch[-1]

    def fetch(first, sources):
        copies = [
            pltpu.make_async_copy(s, refs[first + i], sems.at[first + i])
            for i, s in enumerate(sources)
        ]
        for c in copies:
            c.start()
        for c in copies:
            c.wait()
        return refs[first : first + len(copies)]

    @pl.when(at.mech)
    def _():
        u_in, body_in, mod_in, mask_in = fetch(0, (u, body, mod, mask))
        tile[0:3] = u_in[...]
        tile[3:6] = body_in[...]
        tile[6] = mod_in[...] * mask_in[...].astype(f32)
        pack_rows(at, tile, ya, yb, 7, size_x, size_y)

    @pl.when(~at.mech)
    def _():
        p_in, src_in, sto_in, well_in, host_in = fetch(4, (p, src, sto, well, host))
        where = lane((size_y, 128))
        msg = jnp.zeros((size_y, 128), f32)
        for x in range(size_x):
            diag = 6.0 + sto_in[x] + well_index * well_in[x].astype(f32)
            fields = (p_in[x], relaxation / diag, src_in[x], host_in[x].astype(f32))
            for f, v in enumerate(fields):
                s = z_slot(f, x, size_x)
                msg = jnp.where((where >= s) & (where < s + 6), roll(v, s + 3, 1), msg)
        ya[0:size_y] = msg
        yb[0:size_y] = msg


def count_body(host, out):
    at = Place()
    size_x, size_y = host.shape[0], host.shape[1]
    rows = size_x * size_y

    @pl.when(~at.mech)
    def _():
        high_id, low_id = sub((rows, 128)), sub((128, 128))

        def row(x, y):
            h = host[x, y : y + 1, :]
            left = jnp.where(high_id == (h >> 7), 1.0, 0.0).astype(bf16)
            right = jnp.where(low_id == (h & 127), 1.0, 0.0).astype(bf16)
            return left, right

        out[...] = onehot_sum(size_x, size_y, (rows, 128), row)


def strain_body(tile, xa, xb, ya, yb, xyaa, xyab, xyba, xybb, mask, counts, out, ue):
    at = Place()
    size_x, size_y = mask.shape[0], mask.shape[1]

    @pl.when(at.mech)
    def _():
        for m in range(3):
            for x in range(size_x + 1):
                r = (m * size_x + (x if x < size_x else 0)) * H
                if x < size_x:
                    own = tile[m, x]
                    after = jnp.where(at.yodd, yb[r : r + 1, :], ya[r : r + 1, :])
                else:
                    own = jnp.where(at.xodd, xb[m, 0], xa[m, 0])
                    of_a = jnp.where(at.yodd, xyab[r : r + 1, :], xyaa[r : r + 1, :])
                    of_b = jnp.where(at.yodd, xybb[r : r + 1, :], xyba[r : r + 1, :])
                    after = jnp.where(at.xodd, of_b, of_a)
                    own = jnp.where(at.xnext, own, 0.0)
                    after = jnp.where(at.xnext, after, 0.0)
                ue[m, x, 0:size_y, :] = own
                ue[m, x, size_y : size_y + 8, :] = jnp.zeros((8, 128), f32)
                ue[m, x, size_y : size_y + 1, :] = jnp.where(at.ynext, after, 0.0)
        before = None
        for x in range(size_x + 1):
            v = ue[0, x]
            s = v + z_up(v)
            q0 = s + y_up(s)
            v = ue[1, x]
            s = v + z_up(v)
            q1 = y_up(s) - s
            v = ue[2, x]
            s = z_up(v) - v
            q2 = s + y_up(s)
            if x:
                value = (q0 - before[0]) + (q1 + before[1]) + (q2 + before[2])
                r = (x - 1) * size_y
                out[r : r + size_y, :] = 0.25 * mask[x - 1].astype(f32) * value[0:size_y]
            before = (q0, q1, q2)

    @pl.when(~at.mech)
    def _():
        out[...] = counts[...]


def gather_body(*refs):
    at = Place()
    k = at.groups - 1
    got, refs = refs[:k], refs[k:]
    p, src, sto, well, host = refs[:5]
    tile, xa, xb, ya, yb, xyaa, xyab, xyba, xybb, stiffness = refs[5:15]
    out, out_a, out_b, g0, we, k_high, k_low, ext, acc, table = refs[15:]
    size_x, size_y = p.shape[0], p.shape[1]
    rows = size_x * size_y

    def pick(partner, index):
        value = got[0][index]
        for i in range(1, k):
            value = jnp.where((at.g ^ partner) == i + 1, got[i][index], value)
        return value

    @pl.when(~at.mech)
    def _():
        table[...] = pick(at.groups - 1, slice(None))
        godd = lax.rem(at.g, 2) == 1
        msg_a, msg_b = ya[0:size_y], yb[0:size_y]
        before = jnp.where(at.g > 0, jnp.where(godd, msg_a, msg_b), 0.0)
        after = jnp.where(at.g < at.groups - 2, jnp.where(godd, msg_b, msg_a), 0.0)
        spot = lane((size_y, 128))
        zside = jnp.where((spot & 7) < 3, before, after)
        first_host = z_slot(3, 0, size_x)
        zhost = jnp.where(spot >= first_host, zside, 0.0).astype(jnp.int32)
        cells = [host[x] for x in range(size_x)] + [zhost]
        cells = [c[8 * t : 8 * t + 8] for c in cells for t in range(size_y // 8)]
        highs = [c >> 7 for c in cells]
        lows = [c & 127 for c in cells]

        def step(h, values):
            line = jnp.broadcast_to(table[pl.ds(h, 1), :], (8, 128))
            return tuple(
                jnp.where(hi == h, jnp.take_along_axis(line, lo, axis=1, mode="promise_in_bounds"), v)
                for hi, lo, v in zip(highs, lows, values)
            )

        values = lax.fori_loop(0, rows, step, tuple(jnp.zeros((8, 128), f32) for _ in cells), unroll=4)
        per = size_y // 8
        strain = [jnp.concatenate(values[per * i : per * i + per], axis=0) for i in range(size_x + 1)]

        def z_tile(field, x, depth, source):
            value = roll(source, -(z_slot(field, x, size_x) + 3), 1)
            return jnp.where((spot < depth) | (spot >= 128 - depth), value, 0.0)

        for x in range(size_x):
            diag = 6.0 + sto[x] + well_index * well[x].astype(f32)
            out[0, x, :, 0:128] = p[x]
            out[0, x, :, 128:256] = z_tile(0, x, 3, zside)
            out[1, x, :, 0:128] = relaxation / diag
            out[1, x, :, 128:256] = z_tile(1, x, 2, zside)
            out[2, x, :, 0:128] = src[x] - biot_coef * strain[x]
            out[2, x, :, 128:256] = z_tile(2, x, 2, zside) - biot_coef * z_tile(3, x, 2, strain[size_x])
        pack_rows(at, out, out_a, out_b, 3, size_x, size_y)

    @pl.when(at.mech)
    def _():
        extend(at, ext, tile, xa, xb, ya, yb, (xyaa, xyab), (xyba, xybb), 7, size_x, size_y)
        we[...] = ext[6]
        spread_stiffness(stiffness, k_high, k_low)
        add_apply(ext, we, acc, k_high, k_low, 1, size_x + 5)
        for m in range(3):
            for x in range(2, size_x + 5):
                g0[m, x] = ext[3 + m, x] - acc[m, x] - spring_coef * ext[m, x]


def flow_body(tile, xa, xb, ya, yb, xyaa, xyab, xyba, xybb, sto, well, block, basis, host, pressure, sums, ext, work, corr):
    at = Place()
    size_x, size_y = sto.shape[0], sto.shape[1]
    rows = size_x * size_y
    nx = size_x + 2 * H

    @pl.when(~at.mech)
    def _():
        extend(at, ext, tile, xa, xb, ya, yb, (xyaa, xyab), (xyba, xybb), 3, size_x, size_y)

        def around(field, x):
            v = field[x]
            total = field[x + 1] + field[x - 1]
            total = total + y_up(v) + y_down(v)
            return total + roll(v, 1, 1) + roll(v, -1, 1)

        p0 = [ext[0, x] for x in range(nx)]
        p1 = [None] * nx
        for x in range(1, nx - 1):
            p1[x] = (1.0 - relaxation) * p0[x] + ext[1, x] * (ext[2, x] + around(p0, x))
        p2 = [None] * nx
        for x in range(2, nx - 2):
            p2[x] = (1.0 - relaxation) * p1[x] + ext[1, x] * (ext[2, x] + around(p1, x))
        own = slice(TOP, TOP + size_y)
        for x in range(size_x):
            r = slice(x * size_y, (x + 1) * size_y)
            diag = 6.0 + sto[x] + well_index * well[x].astype(f32)
            here = p2[x + H]
            res = (ext[2, x + H] + around(p2, x + H))[own, 0:128] - diag * here[own, 0:128]
            work[0, r, :] = here[own, 0:128]
            work[1, r, :] = res
            work[2, r, :] = diag
        block_ids = sub((NBLK, 128))

        def coarse_row(x, y):
            r = x * size_y + y
            w = basis[pl.ds(r, 8, stride=rows), :]
            res = work[1, pl.ds(r, 1), :]
            diag = work[2, pl.ds(r, 1), :]
            high, low = split(jnp.concatenate([w * res, w * w * diag], axis=0))
            right = jnp.where(block_ids == block[x, y : y + 1, :], 1.0, 0.0).astype(bf16)
            return jnp.concatenate([high, low], axis=0), right

        acc = onehot_sum(size_x, size_y, (32, NBLK), coarse_row)
        corr[...] = jnp.zeros_like(corr)
        corr[:, 0:NBLK] = (acc[0:8] + acc[16:24]) / (1.0 + (acc[8:16] + acc[24:32]))
        lines = [jnp.broadcast_to(corr[j : j + 1, :], (8, 128)) for j in range(8)]
        for x in range(size_x):
            for t in range(size_y // 8):
                ids = block[x, 8 * t : 8 * t + 8, :]
                r = x * size_y + 8 * t
                delta = jnp.zeros((8, 128), f32)
                for j in range(8):
                    got = jnp.take_along_axis(lines[j], ids, axis=1, mode="promise_in_bounds")
                    delta = delta + basis[j * rows + r : j * rows + r + 8, :] * got
                updated = work[0, r : r + 8, :] + delta
                pressure[x, 8 * t : 8 * t + 8, :] = updated
                change = updated - tile[0, x, 8 * t : 8 * t + 8, 0:128]
                high = change.astype(bf16).astype(f32)
                work[0, r : r + 8, :] = high
                work[1, r : r + 8, :] = change - high
        high_id, low_id = sub((rows, 128)), sub((128, 128))

        def sum_row(x, y):
            r = x * size_y + y
            h = host[x, y : y + 1, :]
            hit = high_id == (h >> 7)
            left = [jnp.where(hit, work[i, pl.ds(r, 1), :], 0.0).astype(bf16) for i in range(2)]
            right = jnp.where(low_id == (h & 127), 1.0, 0.0).astype(bf16)
            return jnp.concatenate(left, axis=0), right

        acc = onehot_sum(size_x, size_y, (2 * rows, 128), sum_row)
        sums[...] = acc[0:rows] + acc[rows : 2 * rows]


def element_body(*refs):
    at = Place()
    k = at.groups - 1
    sums, counts, refs = refs[:k], refs[k : 2 * k], refs[2 * k :]
    mask, out, out_a, out_b = refs
    size_x, size_y = mask.shape[0], mask.shape[1]

    @pl.when(at.mech)
    def _():
        for x in range(size_x):
            r = slice(x * size_y, (x + 1) * size_y)
            total = sums[0][r, :]
            count = counts[0][r, :]
            for i in range(1, k):
                total = total + sums[i][r, :]
                count = count + counts[i][r, :]
            out[0, x] = mask[x].astype(f32) * (total / jnp.maximum(count, 1.0))
        pack_rows(at, out, out_a, out_b, 1, size_x, size_y)


def krylov_body(tile, xa, xb, ya, yb, xyaa, xyab, xyba, xybb, g0, we, k_high, k_low, r_out, q_out, scal, ext, res, acc):
    at = Place()
    size_x, size_y = tile.shape[1], tile.shape[2]
    rows = ext.shape[2]
    own = slice(TOP, TOP + size_y)

    @pl.when(at.mech)
    def _():
        extend(at, ext, tile, xa, xb, ya, yb, (xyaa, xyab), (xyba, xybb), 1, size_x, size_y)
        line = sub((rows, 128))
        inside = ((line >= TOP) | at.yprev) & ((line < TOP + size_y) | at.ynext)

        def inside_x(x):
            if x < H:
                return inside & at.xprev
            if x >= H + size_x:
                return inside & at.xnext
            return inside

        before = None
        for x in range(1, size_x + 5):
            e = ext[0, x]
            sz = e + z_down(e)
            ssz = sz + y_down(sz)
            dsz = y_down(sz) - sz
            dz = z_down(e) - e
            sdz = dz + y_down(dz)
            if before is not None:
                f = (before[0] - ssz, before[1] + dsz, before[2] + sdz)
                for m in range(3):
                    value = g0[m, x] + (0.25 * biot_coef) * f[m]
                    res[m, x] = jnp.where(inside_x(x), value, 0.0)
            before = (ssz, dsz, sdz)

        tiles = range(TOP // 8, (TOP + size_y) // 8)
        planes = range(H, H + size_x)
        e22 = add_apply(res, we, acc, k_high, k_low, 2, size_x + 4, (planes, tiles))
        rr = jnp.zeros((8, 128), f32)
        rq = jnp.zeros((8, 128), f32)
        for m in range(3):
            for x in range(H, H + size_x + 1):
                q = jnp.where(inside_x(x), acc[m, x] + spring_coef * res[m, x], 0.0)
                acc[m, x] = q
                if x < H + size_x:
                    for t in range(TOP, TOP + size_y, 8):
                        v = res[m, x, t : t + 8, :]
                        rr = rr + v * v
                        rq = rq + v * q[t : t + 8]
        rr = total_of(rr)
        shift = total_of(rq) / jnp.maximum(rr, 1e-30)
        rq = jnp.zeros((8, 128), f32)
        qq = jnp.zeros((8, 128), f32)
        for m in range(3):
            for x in range(H, H + size_x + 1):
                q = acc[m, x] - shift * res[m, x]
                acc[m, x] = q
                if x < H + size_x:
                    q_out[m, x - H] = q[own]
                    r_out[m, x - H] = res[m, x, own, :]
                    for t in range(TOP, TOP + size_y, 8):
                        v = q[t : t + 8]
                        qq = qq + v * v
                        rq = rq + v * res[m, x, t : t + 8, :]
        rq, qq = total_of(rq), total_of(qq)

        def plane(x, sums):
            uq = stack_tiles(corners(acc, x), tiles)
            ur = stack_tiles(corners(res, x), tiles)
            vq = stiff(k_high, k_low, uq)
            w = jnp.concatenate([we[x, 8 * t : 8 * t + 8, :] for t in tiles], axis=1)
            return tuple(s + w * dots(u, vq) for s, u in zip(sums, (uq, ur)))

        zero = jnp.zeros((8, 128 * len(tiles)), f32)
        e11, e12 = lax.fori_loop(H, H + size_x, plane, (zero, zero))
        e11 = total_of(e11) + spring_coef * qq
        e12 = total_of(e12) + spring_coef * rq
        e22 = total_of(e22) + spring_coef * rr
        line = sub((8, 128))
        value = jnp.zeros((8, 128), f32)
        for i, v in enumerate((rr, shift, rq, qq, e11, e12, e22)):
            value = jnp.where(line == i, v, value)
        if scal.shape[0] == 8:
            scal[...] = value
        else:
            scal[0:8] = jnp.where(at.xodd, 0.0, value)
            scal[8:16] = jnp.where(at.xodd, value, 0.0)


def final_body(*refs):
    at = Place()
    scals, own, r, q, u, updated, pressure, out = refs[:-7], *refs[-7:]

    @pl.when(~at.mech)
    def _():
        out[...] = jnp.zeros_like(out)
        pressure[...] = updated[...]

    @pl.when(at.mech)
    def _():
        pressure[...] = jnp.zeros_like(pressure)
        parts = [s[8 * i : 8 * i + 8] for s in scals for i in range(s.shape[0] // 8)]
        get = lambda part, i: part[i : i + 1]
        total = lambda fn: functools.reduce(lambda a, b: a + b, [fn(p) for p in parts])
        rr = total(lambda p: get(p, 0))
        mean = total(lambda p: get(p, 2) + get(p, 1) * get(p, 0)) / rr

        def shifted(low, mid, high):
            def one(p):
                gap = get(p, 1) - mean
                return get(p, high) + gap * (2.0 * get(p, mid) + gap * get(p, low))

            return total(one)

        qq = shifted(0, 2, 3)
        energy = shifted(6, 5, 4)
        ratio = qq / (mean * mean * rr)
        curve = energy / (mean * mean) - ratio * ratio * mean * rr
        second = ratio * rr / curve
        shift = own[1:2]
        if own.shape[0] == 16:
            shift = jnp.where(at.xodd, own[9:10], shift)
        by_r = 1.0 / mean + second * (ratio - (shift - mean) / mean)
        by_q = -second / mean
        out[...] = u[...] + by_r[None, None] * r[...] + by_q[None, None] * q[...]


def neighbours(tile, msg_a, msg_b, pair=pair_y):
    xa, xb = exchange_x(tile)
    yb = permuted(msg_b, pair(1))
    ya = permuted(msg_a, pair(0))
    xyab, xybb = exchange_x(yb)
    xyaa, xyba = exchange_x(ya)
    return (xa, xb, ya, yb, xyaa, xyab, xyba, xybb)


def local(
    pressure,
    source,
    storage,
    well_mask,
    block_id,
    basis_weight,
    host_elem,
    displacement,
    body_force,
    modulus,
    elem_mask,
    stiffness,
):
    p, src, sto, well = pressure[0], source[0], storage[0], well_mask[0]
    host, block, mask = host_elem[0], block_id[0], elem_mask[0]
    size_x, size_y, size_z = p.shape
    rows = size_x * size_y
    basis = basis_weight[0].reshape(8 * rows, size_z)
    u, body = displacement[0], body_force[0]
    nx, ny = size_x + 2 * H, size_y + 2 * TOP
    kron = jax.ShapeDtypeStruct((8 * stiffness.shape[0],) * 2, bf16)

    msg = (7 * size_x * H, size_z)
    inputs = (displacement[0], body_force[0], modulus[0], mask, p, src, sto, well, host)
    tile, ya, yb = call(
        pack_body,
        "pack",
        [(7, size_x, size_y, size_z), msg, msg],
        p, src, sto, well, host, u, body, modulus[0], mask,
        scratch=[pltpu.VMEM(v.shape, v.dtype) for v in inputs]
        + [pltpu.SemaphoreType.DMA((len(inputs),))],
        space=pltpu.HBM,
    )
    near = neighbours(tile, ya, yb, pair_first)
    (counts,) = call(count_body, "count", [(rows, size_z)], host)
    (line,) = call(
        strain_body,
        "strain",
        [(rows, size_z)],
        tile, *near, mask, counts,
        scratch=[pltpu.VMEM((3, size_x + 1, size_y + 8, size_z), f32)],
    )
    got = star(line)
    msg = (3 * size_x * H, 2 * size_z)
    cells, ya, yb, g0, we, k_high, k_low = call(
        gather_body,
        "gather",
        [(3, size_x, size_y, 2 * size_z), msg, msg, (3, nx, ny, size_z), (nx, ny, size_z), kron, kron],
        *got, p, src, sto, well, host, tile, *near, stiffness,
        scratch=[
            pltpu.VMEM((7, nx, ny, size_z), f32),
            pltpu.VMEM((3, nx, ny, size_z), f32),
            pltpu.VMEM((rows, size_z), f32),
        ],
    )
    near = neighbours(cells, ya, yb)
    updated, sums = call(
        flow_body,
        "flow",
        [(size_x, size_y, size_z), (rows, size_z)],
        cells, *near, sto, well, block, basis, host,
        scratch=[
            pltpu.VMEM((3, nx, ny, 2 * size_z), f32),
            pltpu.VMEM((3, rows, size_z), f32),
            pltpu.VMEM((8, size_z), f32),
        ],
    )
    summed = star(sums)
    msg = (size_x * H, size_z)
    elem, ya, yb = call(
        element_body,
        "element",
        [(1, size_x, size_y, size_z), msg, msg],
        *summed, *got, mask,
    )
    near = neighbours(elem, ya, yb)
    own = (3, size_x, size_y, size_z)
    duo = lax.axis_size("gx") == 2
    r, q, scal = call(
        krylov_body,
        "krylov",
        [own, own, (16 if duo else 8, size_z)],
        elem, *near, g0, we, k_high, k_low,
        scratch=[
            pltpu.VMEM((1, nx, ny, size_z), f32),
            pltpu.VMEM((3, nx, ny, size_z), f32),
            pltpu.VMEM((3, nx, ny, size_z), f32),
        ],
    )
    if duo:
        pair = scal + x_swap(scal)
        n = lax.axis_size("gy")
        scals = [pair] + [permuted(pair, lambda g, x, y: (g, x, y ^ k)) for k in range(1, n)]
    else:
        scals = [lax.all_gather(scal, ("gx", "gy"), tiled=True)]
    pressure_out, moved = call(
        final_body, "final", [p.shape, own], *scals, scal, r, q, u, updated
    )
    return (pressure_out[None], moved[None])


def solution(mesh):
    cell = P("grp", "gx", "gy", None)
    deep = P("grp", None, "gx", "gy", None)
    placed = (cell, cell, cell, cell, cell, deep, cell, deep, deep, cell, cell, P())
    return jax.shard_map(
        local,
        mesh=mesh,
        in_specs=placed,
        out_specs=(cell, deep),
        check_vma=False,
    )
```

```python
import functools
import jax
import jax.numpy as jnp
from jax import lax
from jax.experimental import pallas as pl
from jax.experimental.pallas import tpu as pltpu
from jax.sharding import PartitionSpec as P

NBLK = 64

biot_coef = 1.5
relaxation = 0.8
spring_coef = 0.5
well_index = 4.0

H = 3
TOP = 8
GRANT = 16 * 1024 * 1024
f32 = jnp.float32
bf16 = jnp.bfloat16


ALL = ("grp", "gx", "gy")


def permuted(value, target):
    sizes = [lax.axis_size(a) for a in ALL]
    flat = lambda g, x, y: (g * sizes[1] + x) * sizes[2] + y
    pairs = []
    for g in range(sizes[0]):
        for x in range(sizes[1]):
            for y in range(sizes[2]):
                pairs.append((flat(g, x, y), flat(*target(g, x, y))))
    return lax.ppermute(value, ALL, pairs)


def idle(g, x, y):
    return g, x ^ 1, y


def x_swap(value):
    return permuted(value, idle)


def exchange_x(value):
    n = lax.axis_size("gx")
    got = x_swap(value)
    if n == 2:
        return got, got
    return got, permuted(value, lambda g, x, y: (g, ((x + 1) if x % 2 else (x - 1)) % n, y))


def up_or_down(i, n, kind):
    j = i + 1 if i % 2 == kind else i - 1
    return j if 0 <= j < n else None


def pair_y(kind):
    n = lax.axis_size("gy")

    def target(g, x, y):
        j = up_or_down(y, n, kind)
        return idle(g, x, y) if j is None else (g, x, j)

    return target


def pair_first(kind):
    last = lax.axis_size("grp") - 1
    along_y = pair_y(kind)

    def target(g, x, y):
        if g == last:
            return along_y(g, x, y)
        j = up_or_down(g, last, kind)
        return idle(g, x, y) if j is None else (j, x, y)

    return target


def star(value):
    n = lax.axis_size("grp")

    def meet(k):
        def target(g, x, y):
            return (g ^ k, x, y) if n - 1 in (g, g ^ k) else idle(g, x, y)

        return target

    return [permuted(value, meet(k)) for k in range(1, n)]


def call(body, name, outs, *args, scratch=(), space=pltpu.VMEM):
    vmem = pl.BlockSpec(memory_space=pltpu.VMEM)
    source = pl.BlockSpec(memory_space=space)
    unique, spots = [], []
    for arg in args:
        found = [i for i, other in enumerate(unique) if other is arg]
        if not found:
            unique.append(arg)
        spots.append(found[0] if found else len(unique) - 1)

    def expanded(*refs):
        return body(*[refs[i] for i in spots], *refs[len(unique) :])

    if space is pltpu.HBM:
        unique = [pltpu.with_memory_space_constraint(v, space) for v in unique]
    return pl.pallas_call(
        expanded,
        name=name,
        out_shape=[o if hasattr(o, "dtype") else jax.ShapeDtypeStruct(o, f32) for o in outs],
        in_specs=[source] * len(unique),
        out_specs=[vmem] * len(outs),
        scratch_shapes=list(scratch),
        compiler_params=pltpu.CompilerParams(vmem_limit_bytes=GRANT),
    )(*unique)


class Place:
    def __init__(self):
        self.groups = lax.axis_size("grp")
        self.g = lax.axis_index("grp")
        self.mech = self.g == self.groups - 1
        for name in ("x", "y"):
            n, i = lax.axis_size("g" + name), lax.axis_index("g" + name)
            setattr(self, name + "odd", lax.rem(i, 2) == 1)
            setattr(self, name + "prev", i > 0)
            setattr(self, name + "next", i < n - 1)


def lane(shape):
    return lax.broadcasted_iota(jnp.int32, shape, len(shape) - 1)


def sub(shape):
    return lax.broadcasted_iota(jnp.int32, shape, len(shape) - 2)


def roll(value, shift, axis):
    return pltpu.roll(value, shift % value.shape[axis], axis)


def z_up(value):
    n = value.shape[-1]
    return jnp.where(lane(value.shape) < n - 1, roll(value, -1, value.ndim - 1), 0.0)


def z_down(value):
    return jnp.where(lane(value.shape) > 0, roll(value, 1, value.ndim - 1), 0.0)


def y_up(value):
    return roll(value, -1, value.ndim - 2)


def y_down(value):
    return roll(value, 1, value.ndim - 2)


def send_rows(at, out_a, out_b, first, low, high):
    rows = slice(first, first + low.shape[0])
    out_a[rows, :] = jnp.where(at.yodd, low, high)
    out_b[rows, :] = jnp.where(at.yodd, high, low)


class Near:
    def __init__(self, at, xa, xb, ya, yb, xyaa, xyab, xyba, xybb):
        self.at, self.tiles = at, (xa, xb)
        self.rows_of = {0: (ya, yb), "a": (xyaa, xyab), "b": (xyba, xybb)}
        self.one = lax.axis_size("gx") == 2

    def x_side(self, dx):
        at = self.at
        return (at.xodd, at.xprev) if dx < 0 else (~at.xodd, at.xnext)

    def plane(self, dx, f, x):
        of_a, valid = self.x_side(dx)
        value = self.tiles[0][f, x]
        if not self.one:
            value = jnp.where(of_a, value, self.tiles[1][f, x])
        return jnp.where(valid, value, 0.0)

    def rows(self, dx, dy, first, count):
        at = self.at
        y_of_a, valid = (at.yodd, at.yprev) if dy < 0 else (~at.yodd, at.ynext)

        def of(kind):
            a, b = self.rows_of[kind]
            rows = slice(first, first + count)
            return jnp.where(y_of_a, a[rows, :], b[rows, :])

        if dx == 0:
            return jnp.where(valid, of(0), 0.0)
        x_of_a, x_valid = self.x_side(dx)
        value = of("a")
        if not self.one:
            value = jnp.where(x_of_a, value, of("b"))
        return jnp.where(valid & x_valid, value, 0.0)


def source_plane(x, size_x):
    if x < 0:
        return -1, x + size_x
    return (1, x - size_x) if x >= size_x else (0, x)


def extend(near, ext, tile, fields, size_x, size_y, wide, high):
    rows = ext.shape[2]
    end = TOP + size_y
    for f in range(fields):
        for x in range(-wide, size_x + wide):
            dx, xs = source_plane(x, size_x)
            xe = x + wide
            first = (f * size_x + xs) * high
            ext[f, xe, 0:TOP, :] = jnp.zeros((TOP, 128), f32)
            ext[f, xe, end:rows, :] = jnp.zeros((rows - end, 128), f32)
            ext[f, xe, TOP:end, :] = tile[f, xs] if dx == 0 else near.plane(dx, f, xs)
            ext[f, xe, TOP - high : TOP, :] = near.rows(dx, -1, first, high)
            ext[f, xe, end : end + high, :] = near.rows(dx, 1, first, high)


def merged(value):
    first, last = value[0:8], value[value.shape[0] - 8 :]
    return jnp.where(sub((8, 128)) == 7, first, last)


def middle(value):
    return [value[t : t + 8] for t in range(TOP, value.shape[0] - 8, 8)]


def variants(here):
    up = z_up(here)
    return {(0, 0): here, (0, 1): up, (1, 0): y_up(here), (1, 1): y_up(up)}


class Corners:
    def __init__(self, nodes):
        self.nodes, self.seen = nodes, {}

    def __call__(self, x):
        for k in (x, x + 1):
            if k not in self.seen:
                self.seen[k] = [variants(self.nodes[m, k]) for m in range(3)]
        return [
            self.seen[x + a][m][b, e]
            for a in range(2) for b in range(2) for e in range(2) for m in range(3)
        ]


def stack_tiles(values, with_ends):
    tiles = [([merged(v)] if with_ends else []) + middle(v) for v in values]
    cols = [jnp.concatenate([t[i] for t in tiles], axis=0) for i in range(len(tiles[0]))]
    return jnp.concatenate(cols, axis=1)


def split(value):
    high = value.astype(bf16)
    return high, (value - high.astype(f32)).astype(bf16)


def stiff(k_both, stacked):
    high, low = split(stacked)
    dot = functools.partial(jnp.dot, preferred_element_type=f32)
    n = stacked.shape[0]
    wide = dot(k_both[...], high)
    return (wide[0:n] + wide[n:]) + dot(k_both[0:n, :], low)


def spread_stiffness(stiffness, k_both):
    n = 8 * stiffness.shape[0]
    pick = jnp.where(sub((n, n // 8)) // 8 == lane((n, n // 8)), 1.0, 0.0).astype(bf16)
    keep = (sub((n, n)) & 7) == (lane((n, n)) & 7)
    for i, term in enumerate(split(stiffness[...])):
        tall = jnp.dot(pick, term, preferred_element_type=f32).astype(bf16)
        wide = lax.dot_general(tall, pick, (((1,), (1,)), ((), ())), preferred_element_type=f32)
        k_both[i * n : i * n + n, :] = jnp.where(keep, wide, 0.0).astype(bf16)


def dots(u, v):
    part = u * v
    total = part[0:8]
    for j in range(1, 24):
        total = total + part[8 * j : 8 * j + 8]
    return total


def apply(nodes, weight, k_both, planes, own=()):
    corners = Corners(nodes)
    out = {}
    energy = jnp.zeros((8, 128), f32)
    planes = list(planes)
    for i in range(0, len(planes), 2):
        group = planes[i : i + 2]
        stacks = [stack_tiles(corners(x), True) for x in group]
        width = stacks[0].shape[1]
        v_all = stiff(k_both, jnp.concatenate(stacks, axis=1))
        for k, x in enumerate(group):
            v = v_all[:, k * width : (k + 1) * width]
            w_plane = weight[x]
            w = [merged(w_plane)] + middle(w_plane)

            def entry(j):
                return [w[t] * v[8 * j : 8 * j + 8, 128 * t : 128 * t + 128] for t in range(len(w))]

            def joined(c, m):
                tiles = [p + z_down(q) for p, q in zip(entry(3 * c + m), entry(3 * (c + 1) + m))]
                return jnp.concatenate(tiles + tiles[:1], axis=0)

            for a in range(2):
                for m in range(3):
                    total = joined(4 * a, m) + y_down(joined(4 * a + 2, m))
                    key = (m, x + a)
                    out[key] = out[key] + total if key in out else total
            if x in own:
                for t in range(1, len(w)):
                    cols = slice(128 * t, 128 * t + 128)
                    energy = energy + w[t] * dots(stacks[k][:, cols], v[:, cols])
    return out, energy


def total_of(value):
    return jnp.sum(jnp.sum(value, axis=0, keepdims=True), axis=1, keepdims=True)


def onehot_sum(size_x, size_y, row_fn):
    acc = None
    for x in range(size_x):
        rows = [row_fn(x, y) for y in range(size_y)]
        part = lax.dot_general(
            jnp.concatenate([r[0] for r in rows], axis=1),
            jnp.concatenate([r[1] for r in rows], axis=1),
            (((1,), (1,)), ((), ())),
            preferred_element_type=f32,
        )
        acc = part if acc is None else acc + part
    return acc


def spread_row(row, count):
    return jnp.broadcast_to(row, (16, 128)).astype(bf16) if count == 16 else jnp.concatenate(
        [spread_row(row, 16)] * (count // 16), axis=0
    )


def hits(row, count):
    ids = sub((count, 128)).astype(f32).astype(bf16)
    return ids == spread_row(row.astype(f32), count)


def host_row(host, x, y, size, values):
    h = host[x, y : y + 1, :]
    hit = hits(h >> 7, size)
    zero = jnp.zeros((size, 128), bf16)
    left = [jnp.where(hit, v, zero) for v in values]
    right = jnp.where(hits(h & 127, 128), jnp.ones((128, 128), bf16), jnp.zeros((128, 128), bf16))
    return jnp.concatenate(left, axis=0), right


def z_slot(field, x, size_x):
    return 8 * (field * size_x + x)


def pack_body(p, src, sto, well, host, u, mod, mask, tile, ya, yb, *scratch):
    at = Place()
    size_x, size_y = p.shape[0], p.shape[1]
    refs, sems = scratch[:-1], scratch[-1]

    def fetch(first, sources):
        copies = [
            pltpu.make_async_copy(s, refs[first + i], sems.at[first + i])
            for i, s in enumerate(sources)
        ]
        for c in copies:
            c.start()
        for c in copies:
            c.wait()
        return refs[first : first + len(copies)]

    @pl.when(at.mech)
    def _():
        u_in, mod_in, mask_in = fetch(0, (u, mod, mask))
        tile[0:3] = u_in[...]
        tile[3] = mod_in[...] * mask_in[...].astype(f32)
        for f in range(4):
            for x in range(size_x):
                low, high = tile[f, x, 0:1, :], tile[f, x, size_y - 1 : size_y, :]
                send_rows(at, ya, yb, f * size_x + x, low, high)

    @pl.when(~at.mech)
    def _():
        p_in, src_in, sto_in, well_in, host_in = fetch(3, (p, src, sto, well, host))
        where = lane((size_y, 128))
        msg = jnp.zeros((size_y, 128), f32)
        for x in range(size_x):
            diag = 6.0 + sto_in[x] + well_index * well_in[x].astype(f32)
            fields = (p_in[x], relaxation / diag, src_in[x], host_in[x].astype(f32))
            for f, v in enumerate(fields):
                s = z_slot(f, x, size_x)
                msg = jnp.where((where >= s) & (where < s + 6), roll(v, s + 3, 1), msg)
        ya[0:size_y] = msg
        yb[0:size_y] = msg


def count_body(host, out):
    at = Place()
    size_x, size_y = host.shape[0], host.shape[1]
    rows = size_x * size_y

    @pl.when(~at.mech)
    def _():
        one = [jnp.ones((rows, 128), bf16)]
        out[...] = onehot_sum(size_x, size_y, lambda x, y: host_row(host, x, y, rows, one))


def strain_body(tile, *refs):
    at = Place()
    near, (mask, counts, out, ue) = Near(at, *refs[:8]), refs[8:]
    size_x, size_y = mask.shape[0], mask.shape[1]

    @pl.when(at.mech)
    def _():
        for m in range(3):
            for x in range(size_x + 1):
                dx, xs = source_plane(x, size_x)
                ue[m, x, 0:size_y, :] = tile[m, xs] if dx == 0 else near.plane(dx, m, xs)
                ue[m, x, size_y : size_y + 8, :] = jnp.zeros((8, 128), f32)
                ue[m, x, size_y : size_y + 1, :] = near.rows(dx, 1, m * size_x + xs, 1)
        before = None
        for x in range(size_x + 1):
            v = ue[0, x]
            s = v + z_up(v)
            q0 = s + y_up(s)
            v = ue[1, x]
            s = v + z_up(v)
            q1 = y_up(s) - s
            v = ue[2, x]
            s = z_up(v) - v
            q2 = s + y_up(s)
            if x:
                value = (q0 - before[0]) + (q1 + before[1]) + (q2 + before[2])
                r = (x - 1) * size_y
                out[r : r + size_y, :] = 0.25 * mask[x - 1].astype(f32) * value[0:size_y]
            before = (q0, q1, q2)

    @pl.when(~at.mech)
    def _():
        out[...] = counts[...]


def z_fold(values, size_x):
    spot = lane(values[0].shape)
    out = jnp.zeros(values[0].shape, f32)
    for i, v in enumerate(values):
        out = jnp.where((spot >= 8 * i) & (spot < 8 * i + 6), roll(v, 8 * i + 3, 1), out)
    return out


def z_unfold(value, i, depth):
    spot = lane(value.shape)
    return jnp.where((spot < depth) | (spot >= 128 - depth), roll(value, -(8 * i + 3), 1), 0.0)


def gather_body(*refs):
    at = Place()
    k = at.groups - 1
    got, refs = refs[:k], refs[k:]
    p, src, sto, well, host, body, stiffness, tile = refs[:8]
    near, ya, yb = Near(at, *refs[8:16]), refs[10], refs[11]
    out, out_a, out_b, k_both, shift, ext, table, cells = refs[16:]
    size_x, size_y = p.shape[0], p.shape[1]
    rows = size_x * size_y

    @pl.when(~at.mech)
    def _():
        value = got[0][...]
        for i in range(1, k):
            value = jnp.where((at.g ^ k) == i + 1, got[i][...], value)
        table[...] = value
        godd = lax.rem(at.g, 2) == 1
        msg_a, msg_b = ya[0:size_y], yb[0:size_y]
        before = jnp.where(at.g > 0, jnp.where(godd, msg_a, msg_b), 0.0)
        after = jnp.where(at.g < at.groups - 2, jnp.where(godd, msg_b, msg_a), 0.0)
        spot = lane((size_y, 128))
        zside = jnp.where((spot & 7) < 3, before, after)
        first_host = 8 * (3 * size_x)
        for x in range(size_x):
            cells[x * size_y : (x + 1) * size_y] = host[x]
        cells[rows : rows + size_y] = jnp.where(spot >= first_host, zside, 0.0).astype(jnp.int32)

        def step(i, carry):
            here = pl.ds(pl.multiple_of(8 * i, 8), 8)
            index = cells[here, :]
            high, low = index >> 7, index & 127
            parts = [jnp.zeros((8, 128), f32) for _ in range(4)]
            for h in range(rows):
                line = jnp.broadcast_to(table[h : h + 1, :], (8, 128))
                found = jnp.take_along_axis(line, low, axis=1, mode="promise_in_bounds")
                parts[h % 4] = jnp.where(high == h, found, parts[h % 4])
            ext[0, 0, here, :] = (parts[0] + parts[1]) + (parts[2] + parts[3])
            return carry

        lax.fori_loop(0, (rows + size_y) // 8, step, 0)
        zstrain = ext[0, 0, rows : rows + size_y, :]
        for x in range(size_x):
            diag = 6.0 + sto[x] + well_index * well[x].astype(f32)
            strain = ext[0, 0, x * size_y : (x + 1) * size_y, :]
            out[0, x] = p[x]
            out[1, x] = relaxation / diag
            out[2, x] = src[x] - biot_coef * strain
            out[3, x] = z_unfold(zside, x, 3)
            out[4, x] = z_unfold(zside, size_x + x, 2)
            zforce = z_unfold(zside, 2 * size_x + x, 2)
            out[5, x] = zforce - biot_coef * z_unfold(zstrain, 3 * size_x + x, 2)
        low, high = slice(0, H), slice(size_y - H, size_y)
        for f in range(3):
            for x in range(size_x):
                send_rows(at, out_a, out_b, (f * size_x + x) * H, out[f, x, low, :], out[f, x, high, :])
        fold = [
            z_fold([out[3 + f, x, side, :] for f in range(3) for x in range(size_x)], size_x)
            for side in (low, high)
        ]
        send_rows(at, out_a, out_b, 3 * size_x * H, *fold)

    @pl.when(at.mech)
    def _():
        spread_stiffness(stiffness, k_both)
        nodes = ext.at[:, 0 : size_x + 2, 0 : size_y + 2 * TOP]
        extend(near, nodes, tile, 4, size_x, size_y, 1, 1)
        image, _ = apply(nodes, nodes.at[3], k_both, range(size_x + 1))
        own = slice(TOP, TOP + size_y)
        weight = jnp.zeros((8, 128), f32)
        for x in range(size_x):
            for m in range(3):
                u = tile[m, x]
                out[m, x] = body[m, x] - image[m, x + 1][own] - spring_coef * u
            out[3, x] = tile[3, x]
            for t in range(0, size_y, 8):
                weight = weight + tile[3, x, t : t + 8, :]
        n = stiffness.shape[0]
        trace = total_of(jnp.where(sub((n, n)) == lane((n, n)), stiffness[...], 0.0))
        mean = total_of(weight) * trace / (3.0 * rows * 128.0)
        shift[...] = jnp.broadcast_to(mean + spring_coef, (8, 128))
        for f in range(4):
            for x in range(size_x):
                low, high = out[f, x, 0:2, :], out[f, x, size_y - 2 : size_y, :]
                send_rows(at, out_a, out_b, (f * size_x + x) * 2, low, high)


def flow_body(tile, *refs):
    at = Place()
    near, refs = Near(at, *refs[:8]), refs[8:]
    sto, well, block, basis, host, pressure, sums, mech, ext, work, corr = refs
    size_x, size_y = sto.shape[0], sto.shape[1]
    rows = size_x * size_y
    nx = size_x + 2 * H

    @pl.when(at.mech)
    def _():
        extend(near, mech, tile, 4, size_x, size_y, 2, 2)

    @pl.when(~at.mech)
    def _():
        main = ext.at[:, :, :, 0:128]
        extend(near, main, tile, 3, size_x, size_y, H, H)
        first = 3 * size_x * H
        end = TOP + size_y
        for x in range(-H, size_x + H):
            dx, xs = source_plane(x, size_x)
            below, above = near.rows(dx, -1, first, H), near.rows(dx, 1, first, H)
            for f in range(3):
                i = f * size_x + xs
                xe = x + H
                ext[f, xe, 0:TOP, 128:256] = jnp.zeros((TOP, 128), f32)
                ext[f, xe, end : end + TOP, 128:256] = jnp.zeros((TOP, 128), f32)
                own = tile[3 + f, xs] if dx == 0 else near.plane(dx, 3 + f, xs)
                ext[f, xe, TOP:end, 128:256] = own
                ext[f, xe, TOP - H : TOP, 128:256] = z_unfold(below, i, H)
                ext[f, xe, end : end + H, 128:256] = z_unfold(above, i, H)

        def around(field, x):
            v = field[x]
            total = field[x + 1] + field[x - 1]
            total = total + y_up(v) + y_down(v)
            return total + roll(v, 1, 1) + roll(v, -1, 1)

        p0 = [ext[0, x] for x in range(nx)]
        p1 = [None] * nx
        for x in range(1, nx - 1):
            p1[x] = (1.0 - relaxation) * p0[x] + ext[1, x] * (ext[2, x] + around(p0, x))
        p2 = [None] * nx
        for x in range(2, nx - 2):
            p2[x] = (1.0 - relaxation) * p1[x] + ext[1, x] * (ext[2, x] + around(p1, x))
        own = slice(TOP, TOP + size_y)
        for x in range(size_x):
            r = slice(x * size_y, (x + 1) * size_y)
            diag = 6.0 + sto[x] + well_index * well[x].astype(f32)
            here = p2[x + H]
            res = (ext[2, x + H] + around(p2, x + H))[own, 0:128] - diag * here[own, 0:128]
            work[0, r, :] = here[own, 0:128]
            work[1, r, :] = res
            work[2, r, :] = diag
        one, zero = jnp.ones((NBLK, 128), bf16), jnp.zeros((NBLK, 128), bf16)

        def coarse_row(x, y):
            r = x * size_y + y
            w = basis[pl.ds(r, 8, stride=rows), :]
            res, diag = work[1, r : r + 1, :], work[2, r : r + 1, :]
            high, low = split(jnp.concatenate([w * res, w * w * diag], axis=0))
            right = jnp.where(hits(block[x, y : y + 1, :], NBLK), one, zero)
            return jnp.concatenate([high, low], axis=0), right

        acc = onehot_sum(size_x, size_y, coarse_row)
        corr[...] = jnp.zeros_like(corr)
        corr[:, 0:NBLK] = (acc[0:8] + acc[16:24]) / (1.0 + (acc[8:16] + acc[24:32]))
        lines = [jnp.broadcast_to(corr[j : j + 1, :], (8, 128)) for j in range(8)]
        for x in range(size_x):
            for t in range(size_y // 8):
                ids = block[x, 8 * t : 8 * t + 8, :]
                r = x * size_y + 8 * t
                delta = jnp.zeros((8, 128), f32)
                for j in range(8):
                    got = jnp.take_along_axis(lines[j], ids, axis=1, mode="promise_in_bounds")
                    delta = delta + basis[j * rows + r : j * rows + r + 8, :] * got
                updated = work[0, r : r + 8, :] + delta
                pressure[x, 8 * t : 8 * t + 8, :] = updated
                change = updated - tile[0, x, 8 * t : 8 * t + 8, :]
                high = change.astype(bf16).astype(f32)
                work[0, r : r + 8, :] = high
                work[1, r : r + 8, :] = change - high

        def sum_row(x, y):
            r = x * size_y + y
            values = [spread_row(work[i, r : r + 1, :], rows) for i in range(2)]
            return host_row(host, x, y, rows, values)

        acc = onehot_sum(size_x, size_y, sum_row)
        sums[...] = acc[0:rows] + acc[rows : 2 * rows]


def element_body(*refs):
    at = Place()
    k = at.groups - 1
    sums, counts, refs = refs[:k], refs[k : 2 * k], refs[2 * k :]
    mask, out, out_a, out_b = refs
    size_x, size_y = mask.shape[0], mask.shape[1]

    @pl.when(at.mech)
    def _():
        for x in range(size_x):
            r = slice(x * size_y, (x + 1) * size_y)
            total = sums[0][r, :]
            count = counts[0][r, :]
            for i in range(1, k):
                total = total + sums[i][r, :]
                count = count + counts[i][r, :]
            out[0, x] = mask[x].astype(f32) * (total / jnp.maximum(count, 1.0))
        for x in range(size_x):
            send_rows(at, out_a, out_b, 2 * x, out[0, x, 0:2, :], out[0, x, size_y - 2 : size_y, :])


def krylov_body(tile, *refs):
    at = Place()
    near, (mech, k_both, shift, r_out, q_out, scal, ext, res, acc) = Near(at, *refs[:8]), refs[8:]
    size_x, size_y = tile.shape[1], tile.shape[2]
    rows = ext.shape[2]
    own = slice(TOP, TOP + size_y)

    @pl.when(at.mech)
    def _():
        extend(near, ext, tile, 1, size_x, size_y, 2, 2)
        line = sub((rows, 128))
        inside = ((line >= TOP) | at.yprev) & ((line < TOP + size_y) | at.ynext)

        def inside_x(x):
            if x < 2:
                return inside & at.xprev
            return inside & at.xnext if x >= 2 + size_x else inside

        before = None
        for x in range(size_x + 4):
            e = ext[0, x]
            sz = e + z_down(e)
            szd = y_down(sz)
            dz = z_down(e) - e
            now = (szd + sz, szd - sz, dz + y_down(dz))
            if before is not None:
                f = (before[0] - now[0], before[1] + now[1], before[2] + now[2])
                for m in range(3):
                    value = mech[m, x] + (0.25 * biot_coef) * f[m]
                    res[m, x] = jnp.where(inside_x(x), value, 0.0)
            before = now

        weight = mech.at[3]
        planes = range(2, 2 + size_x)
        image, e22 = apply(res, weight, k_both, range(1, size_x + 3), planes)
        gap = spring_coef - shift[0:1, :]
        rr = jnp.zeros((8, 128), f32)
        rq, qq = rr, rr
        for m in range(3):
            for x in range(2, size_x + 3):
                r = res[m, x]
                q = jnp.where(inside_x(x), image[m, x] + gap * r, 0.0)
                acc[m, x] = q
                if x in planes:
                    q_out[m, x - 2] = q[own]
                    r_out[m, x - 2] = r[own]
                    for t in range(TOP, TOP + size_y, 8):
                        rt, qt = r[t : t + 8], q[t : t + 8]
                        rr = rr + rt * rt
                        rq = rq + rt * qt
                        qq = qq + qt * qt
        of_q, of_r = Corners(acc), Corners(res)
        e11 = jnp.zeros((8, 128), f32)
        e12 = e11
        for x in planes:
            uq = stack_tiles(of_q(x), False)
            ur = stack_tiles(of_r(x), False)
            vq = stiff(k_both, uq)
            for t, w in enumerate(middle(weight[x])):
                cols = slice(128 * t, 128 * t + 128)
                e11 = e11 + w * dots(uq[:, cols], vq[:, cols])
                e12 = e12 + w * dots(ur[:, cols], vq[:, cols])
        e11 = e11 + spring_coef * qq
        e12 = e12 + spring_coef * rq
        e22 = e22 + spring_coef * rr
        line = sub((8, 128))
        value = jnp.where(line == 1, shift[...], 0.0)
        for i, v in ((0, rr), (2, rq), (3, qq), (4, e11), (5, e12), (6, e22)):
            value = jnp.where(line == i, total_of(v), value)
        if scal.shape[0] == 8:
            scal[...] = value
        else:
            scal[0:8] = jnp.where(at.xodd, 0.0, value)
            scal[8:16] = jnp.where(at.xodd, value, 0.0)


def final_body(*refs):
    at = Place()
    scals, own, r, q, u, updated, pressure, out = refs[:-7], *refs[-7:]

    @pl.when(~at.mech)
    def _():
        out[...] = jnp.zeros_like(out)
        pressure[...] = updated[...]

    @pl.when(at.mech)
    def _():
        pressure[...] = jnp.zeros_like(pressure)
        parts = [s[8 * i : 8 * i + 8] for s in scals for i in range(s.shape[0] // 8)]
        get = lambda part, i: part[i : i + 1]
        total = lambda fn: functools.reduce(lambda a, b: a + b, [fn(p) for p in parts])
        rr = total(lambda p: get(p, 0))
        mean = total(lambda p: get(p, 2) + get(p, 1) * get(p, 0)) / rr

        def shifted(low, mid, high):
            def one(p):
                gap = get(p, 1) - mean
                return get(p, high) + gap * (2.0 * get(p, mid) + gap * get(p, low))

            return total(one)

        qq = shifted(0, 2, 3)
        energy = shifted(6, 5, 4)
        ratio = qq / (mean * mean * rr)
        curve = energy / (mean * mean) - ratio * ratio * mean * rr
        second = ratio * rr / curve
        shift = own[1:2]
        if own.shape[0] == 16:
            shift = jnp.where(at.xodd, own[9:10], shift)
        by_r = 1.0 / mean + second * (ratio - (shift - mean) / mean)
        by_q = -second / mean
        out[...] = u[...] + by_r[None, None] * r[...] + by_q[None, None] * q[...]


def neighbours(tile, msg_a, msg_b, pair=pair_y):
    xa, xb = exchange_x(tile)
    yb = permuted(msg_b, pair(1))
    ya = permuted(msg_a, pair(0))
    xyab, xybb = exchange_x(yb)
    xyaa, xyba = exchange_x(ya)
    return (xa, xb, ya, yb, xyaa, xyab, xyba, xybb)


def local(
    pressure,
    source,
    storage,
    well_mask,
    block_id,
    basis_weight,
    host_elem,
    displacement,
    body_force,
    modulus,
    elem_mask,
    stiffness,
):
    p, src, sto, well = pressure[0], source[0], storage[0], well_mask[0]
    host, block, mask = host_elem[0], block_id[0], elem_mask[0]
    size_x, size_y, size_z = p.shape
    rows = size_x * size_y
    basis = basis_weight[0].reshape(8 * rows, size_z)
    u, body = displacement[0], body_force[0]
    nx, ny = size_x + 2 * H, size_y + 2 * TOP
    cell = (size_x, size_y, size_z)

    msg = (max(4 * size_x, size_y), size_z)
    inputs = (displacement[0], modulus[0], mask, p, src, sto, well, host)
    tile, ya, yb = call(
        pack_body,
        "pack",
        [(4, *cell), msg, msg],
        p, src, sto, well, host, u, modulus[0], mask,
        scratch=[pltpu.VMEM(v.shape, v.dtype) for v in inputs]
        + [pltpu.SemaphoreType.DMA((len(inputs),))],
        space=pltpu.HBM,
    )
    near = neighbours(tile, ya, yb, pair_first)
    (counts,) = call(count_body, "count", [(rows, size_z)], host)
    (line,) = call(
        strain_body,
        "strain",
        [(rows, size_z)],
        tile, *near, mask, counts,
        scratch=[pltpu.VMEM((3, size_x + 1, size_y + 8, size_z), f32)],
    )
    got = star(line)
    msg = (3 * size_x * H + 4, size_z)
    n = 8 * stiffness.shape[0]
    k_shape = jax.ShapeDtypeStruct((2 * n, n), bf16)
    cells, ya, yb, k_both, shift = call(
        gather_body,
        "gather",
        [(6, *cell), msg, msg, k_shape, (8, size_z)],
        *got, p, src, sto, well, host, body, stiffness, tile, *near,
        scratch=[
            pltpu.VMEM((4, size_x + 2, max(ny, rows + size_y), size_z), f32),
            pltpu.VMEM((rows, size_z), f32),
            pltpu.VMEM((rows + size_y, size_z), jnp.int32),
        ],
    )
    near = neighbours(cells, ya, yb)
    updated, sums, mech = call(
        flow_body,
        "flow",
        [cell, (rows, size_z), (4, size_x + 4, ny, size_z)],
        cells, *near, sto, well, block, basis, host,
        scratch=[
            pltpu.VMEM((3, nx, ny, 2 * size_z), f32),
            pltpu.VMEM((3, rows, size_z), f32),
            pltpu.VMEM((8, size_z), f32),
        ],
    )
    summed = star(sums)
    msg = (2 * size_x, size_z)
    elem, ya, yb = call(
        element_body,
        "element",
        [(1, *cell), msg, msg],
        *summed, *got, mask,
    )
    near = neighbours(elem, ya, yb)
    own = (3, *cell)
    duo = lax.axis_size("gx") == 2
    r, q, scal = call(
        krylov_body,
        "krylov",
        [own, own, (16 if duo else 8, size_z)],
        elem, *near, mech, k_both, shift,
        scratch=[
            pltpu.VMEM((1, size_x + 4, ny, size_z), f32),
            pltpu.VMEM((3, size_x + 4, ny, size_z), f32),
            pltpu.VMEM((3, size_x + 4, ny, size_z), f32),
        ],
    )
    if duo:
        pair = scal + x_swap(scal)
        scals = [pair] + [
            permuted(pair, lambda g, x, y: (g, x, y ^ k)) for k in range(1, lax.axis_size("gy"))
        ]
    else:
        scals = [lax.all_gather(scal, ("gx", "gy"), tiled=True)]
    pressure_out, moved = call(
        final_body, "final", [p.shape, own], *scals, scal, r, q, u, updated
    )
    return (pressure_out[None], moved[None])


def solution(mesh):
    cell = P("grp", "gx", "gy", None)
    deep = P("grp", None, "gx", "gy", None)
    placed = (cell, cell, cell, cell, cell, deep, cell, deep, deep, cell, cell, P())
    return jax.shard_map(
        local,
        mesh=mesh,
        in_specs=placed,
        out_specs=(cell, deep),
        check_vma=False,
    )
```
